128 devices in a mesh: tm: 32 (over z, x, core), space: 4 (over y).
Axes of the slice: x: 4, y: 4, z: 4, core: 2. Of those that a mesh axis runs over, the one named last changes fastest.
Arguments:
- snapshots: bfloat16 [1024, 3, 131072], P('tm', None, 'space'), may hold values from -12 to 12
- cell_weights: float32 [131072], P('space'), may hold values from 0.2 to 5
- freq_order: int32 [32], replicated, may hold values from 0 to 31, each once
Outputs:
- energies: float32 [32, 4], P('tm')
- modes: bfloat16 [32, 4, 2, 3, 131072], P('tm', None, None, None, 'space')
The draws below stay inside these ranges and needn't reach their ends.
All inputs are finite; a program needn't handle non-finite values.
Results may differ from the reference program's by a relative error of at most 0.0043.
Values may be sent and summed in bfloat16 or wider, within the bound.
A program may use at most 192 MiB of HBM per device.

```python
import math
import jax
import jax.numpy as jnp
from jax import lax

NFFT = 64
COMP = 3
MODES = 4
SWEEPS = 3
HALF = 32
NF = 32
SNAPS = 1024
NB = 31
CELLS = 131072
N_TM = 32


def draw_snapshots(key, part):
    noise_key = jax.random.fold_in(jax.random.fold_in(key, 7), 0)
    rate_key = jax.random.fold_in(jax.random.fold_in(key, 7), 1)
    shape_key = jax.random.fold_in(jax.random.fold_in(key, 7), 2)
    level_key = jax.random.fold_in(jax.random.fold_in(key, 7), 4)
    time_axis = jnp.arange(SNAPS, dtype=jnp.float32)[:, None]
    base_rates = jnp.arange(NF, dtype=jnp.float32)[None, :]
    wave_rates = base_rates + jax.random.uniform(rate_key, (1, NF), jnp.float32, -0.35, 0.35)
    angle_rows = 2.0 * math.pi * wave_rates * time_axis / NFFT
    temporal = jnp.concatenate([jnp.cos(angle_rows), jnp.sin(angle_rows)], 1)
    levels = jnp.exp(jax.random.uniform(level_key, (NF,), jnp.float32, math.log(0.15), math.log(0.45)))
    level_rows = jnp.concatenate([levels, levels], 0)[:, None]
    spatial = level_rows * jax.random.normal(shape_key, (2 * NF, COMP * CELLS), jnp.float32)
    coherent = jnp.dot(temporal, spatial, precision=lax.Precision.HIGHEST).reshape(SNAPS, COMP, CELLS)
    noise_part = jax.random.normal(noise_key, (SNAPS, COMP, CELLS), jnp.float32)
    velocity = noise_part + coherent
    return jnp.clip(velocity, -12.0, 12.0).astype(jnp.bfloat16)


def block_scale(rng, extent, cuts, least, largest):
    gain, own = 1.0, jax.random.fold_in(rng, 6)
    for position, shards_of in cuts:
        steps = jnp.exp(jax.random.uniform(jax.random.fold_in(own, position), (shards_of,), jnp.float32, least / len(cuts), largest / len(cuts)))
        gain = gain * jnp.repeat(steps, extent[position] // shards_of).reshape([-1 if axis == position else 1 for axis in range(len(extent))])
    return gain


def setup_inputs(seed: int = 0) -> dict:
    splits = jax.random.split(jax.random.key(seed), 4)
    snapshots = draw_snapshots(jax.random.fold_in(splits[3], 71), 0)
    cell_weights = jnp.clip(jnp.exp(math.log(5.0) - 3.218876 * jax.random.uniform(splits[1], (CELLS,), jnp.float32) ** block_scale(splits[1], (CELLS,), ((0, 4),), -0.2, 0.2)), 0.2, 5.0)
    freq_order = jax.random.permutation(splits[2], NF).astype(jnp.int32)
    return dict(snapshots=snapshots, cell_weights=cell_weights, freq_order=freq_order)


shift_rate = 0.61
top_precision = lax.Precision.HIGHEST

def window_tables():
    sample = jnp.arange(NFFT, dtype=jnp.int32)
    freq_rows = jnp.arange(NF, dtype=jnp.int32)
    turn_index = (freq_rows[:, None] * sample[None, :] % NFFT).astype(jnp.float32)
    angle_grid = 2.0 * math.pi * turn_index / NFFT
    hann_window = 0.5 - 0.5 * jnp.cos(2.0 * math.pi * sample.astype(jnp.float32) / NFFT)
    dft_basis = jnp.stack([hann_window * jnp.cos(angle_grid), -hann_window * jnp.sin(angle_grid)], 0)
    return (dft_basis.astype(jnp.bfloat16), jnp.sum(hann_window * hann_window))

def start_vectors(block_count):
    rows_idx = jnp.arange(block_count, dtype=jnp.float32)[:, None] + 1.0
    cols_idx = jnp.arange(MODES, dtype=jnp.float32)[None, :] + 1.0
    return jnp.cos(shift_rate * rows_idx * cols_idx)

def complex_apply(real_part, imag_part, vec_re, vec_im):
    first_re = jnp.einsum('fab,fbk->fak', real_part, vec_re, precision=top_precision)
    first_im = jnp.einsum('fab,fbk->fak', imag_part, vec_im, precision=top_precision)
    cross_re = jnp.einsum('fab,fbk->fak', real_part, vec_im, precision=top_precision)
    cross_im = jnp.einsum('fab,fbk->fak', imag_part, vec_re, precision=top_precision)
    return (first_re - first_im, cross_re + cross_im)

def orthonormal(image_re, image_im):
    done_re = []
    done_im = []
    for column in range(MODES):
        col_re = image_re[:, :, column]
        col_im = image_im[:, :, column]
        for earlier in range(column):
            prev_re = done_re[earlier]
            prev_im = done_im[earlier]
            inner_re = lax.optimization_barrier(jnp.sum(prev_re * col_re + prev_im * col_im, axis=1, keepdims=True))
            inner_im = lax.optimization_barrier(jnp.sum(prev_re * col_im - prev_im * col_re, axis=1, keepdims=True))
            col_re = col_re - (inner_re * prev_re - inner_im * prev_im)
            col_im = col_im - (inner_re * prev_im + inner_im * prev_re)
        length = jnp.sqrt(lax.optimization_barrier(jnp.sum(col_re * col_re + col_im * col_im, axis=1, keepdims=True)))
        done_re.append(col_re / length)
        done_im.append(col_im / length)
    return (jnp.stack(done_re, 2), jnp.stack(done_im, 2))

def power_sweeps(real_part, imag_part):
    start_table = start_vectors(real_part.shape[-1])
    vec_re = jnp.broadcast_to(start_table, real_part.shape[:1] + start_table.shape)
    vec_im = jnp.zeros_like(vec_re)
    for sweep_step in range(SWEEPS):
        image_re, image_im = complex_apply(real_part, imag_part, vec_re, vec_im)
        vec_re, vec_im = orthonormal(image_re, image_im)
    applied_re, applied_im = complex_apply(real_part, imag_part, vec_re, vec_im)
    energy = lax.optimization_barrier(jnp.sum(vec_re * applied_re + vec_im * applied_im, axis=1))
    return (vec_re, vec_im, energy)

def mixing_rows(vec_re, vec_im, factor):
    turned_re = jnp.swapaxes(vec_re, 1, 2) * factor
    turned_im = jnp.swapaxes(vec_im, 1, 2) * factor
    real_out = jnp.stack([turned_re, -turned_im], 2)
    imag_out = jnp.stack([turned_im, turned_re], 2)
    return jnp.stack([real_out, imag_out], 2).astype(jnp.bfloat16)

def reference(snapshots, cell_weights, freq_order):
    dft_basis, energy_sum = window_tables()
    gram_scale = 1.0 / (energy_sum * (COMP * CELLS))
    factor = 1.0 / jnp.sqrt(energy_sum)
    time_rows = snapshots.reshape(N_TM, HALF, COMP * CELLS).transpose(1, 0, 2).reshape(HALF, N_TM * COMP * CELLS)
    point_weights = jnp.tile(cell_weights, COMP)

    def one_frequency(frequency):
        basis_rows = dft_basis[:, frequency, :]
        split_basis = jnp.concatenate([basis_rows[:, :HALF], basis_rows[:, HALF:]], 0)
        halves_out = jnp.dot(split_basis, time_rows, preferred_element_type=jnp.float32).reshape(4, N_TM, COMP * CELLS)
        spectra = (halves_out[0:2, :-1] + halves_out[2:4, 1:]).astype(jnp.bfloat16)
        weighted = (spectra.astype(jnp.float32) * point_weights).astype(jnp.bfloat16)
        products = jnp.dot(weighted.reshape(2 * NB, -1), spectra.reshape(2 * NB, -1).T, preferred_element_type=jnp.float32).reshape(2, NB, 2, NB)
        gram_re = (products[0, :, 0] + products[1, :, 1]) * gram_scale
        gram_im = (products[0, :, 1] - products[1, :, 0]) * gram_scale
        vec_re, vec_im, energy = power_sweeps(gram_re[None], gram_im[None])
        mixing = mixing_rows(vec_re, vec_im, factor)[0].reshape(2 * MODES, 2 * NB)
        mode_rows = jnp.dot(mixing, spectra.reshape(2 * NB, -1), preferred_element_type=jnp.float32)
        return (energy[0], mode_rows.astype(jnp.bfloat16).reshape(MODES, 2, COMP, CELLS))
    energies, modes = lax.map(one_frequency, freq_order)
    return (energies, modes)
```

```python
import functools
import math

import jax
import jax.numpy as jnp
import numpy as np
from jax import lax
from jax.experimental import pallas as pl
from jax.experimental.pallas import tpu as pltpu
from jax.sharding import PartitionSpec as P

NFFT = 64
COMP = 3
MODES = 4
SWEEPS = 3
HALF = 32
NF = 32
NB = 31
SHIFT = 0.61
MESH = pl.DeviceIdType.MESH

CYCLE = (0, 1, 2, 3)
PEERS = [
    (CYCLE[(turn + lead) % 4], dx, dc)
    for dc in (0, 1)
    for turn in range(4)
    for dx, lead in ((2, 0), (1, 1), (3, 3), (0, 2))
    if (CYCLE[(turn + lead) % 4], dx, dc) != (0, 0, 0)
]
GROUPS = 8
IN_GROUP = NF // GROUPS
GROUP_ROWS = IN_GROUP * 2 * HALF
GROUP_ORDER = (0, 2, 6, 4, 1, 3, 7, 5)


def peer_of(me, offset):
    z, x, core = me // 8, (me // 2) % 4, me % 2
    return (((z + offset[0]) % 4) * 4 + (x + offset[1]) % 4) * 2 + (core + offset[2]) % 2


def basis_rows():
    sample = np.arange(NFFT)
    freqs = np.arange(NF)
    turn = ((freqs[:, None] * sample[None, :]) % NFFT).astype(np.float32)
    angle = np.float32(2.0 * math.pi) * turn / np.float32(NFFT)
    hann_angle = np.float32(2.0 * math.pi) * sample.astype(np.float32) / np.float32(NFFT)
    hann = np.float32(0.5) - np.float32(0.5) * np.cos(hann_angle)
    basis = np.stack([hann * np.cos(angle), -hann * np.sin(angle)], 1)
    even = np.concatenate([basis, basis], 2)
    odd = np.concatenate([basis[:, :, HALF:], basis, basis[:, :, :HALF]], 2)
    table = np.zeros((NF, 8, 128), np.float32)
    table[:, 0:2] = even
    table[:, 2:4] = odd
    return table, float(np.sum(hann * hann))


def first_vectors():
    rows = np.arange(NB, dtype=np.float32)[:, None] + np.float32(1.0)
    cols = np.arange(MODES, dtype=np.float32)[None, :] + np.float32(1.0)
    table = np.zeros((2 * HALF, 128), np.float32)
    table[:NB, :MODES] = np.cos(np.float32(SHIFT) * rows * cols)
    return table


def turned(y):
    return jnp.concatenate([y[HALF:], -y[:HALF]], axis=0)


def lane_halves_swapped(x, lane):
    return jnp.where(lane < HALF, pltpu.roll(x, 128 - HALF, 1), pltpu.roll(x, HALF, 1))


def kernel(
    parts, width, scale, factor,
    order, snaps, weights, table, start, energies, modes,
    x_buf, dft, spec, gram, gram_out, gram_in, total, mix, out_buf,
    x_send, x_recv, g_send, g_recv, y_send, y_recv, m_send, m_recv, o_send, o_recv,
):
    me = lax.axis_index("tm")
    row = lax.axis_index("space")
    n_space = lax.axis_size("space")
    own = parts * width

    barrier = pltpu.get_barrier_semaphore()
    for offset in PEERS:
        pl.semaphore_signal(
            barrier, inc=1, device_id={"tm": peer_of(me, offset)}, device_id_type=MESH
        )
    for step in range(1, n_space):
        pl.semaphore_signal(
            barrier, inc=1, device_id={"space": lax.rem(row + step, n_space)}, device_id_type=MESH
        )
    pl.semaphore_wait(barrier, len(PEERS) + n_space - 1)

    def source(owner, part):
        at = pl.multiple_of(owner * own + part * width, width)
        return snaps.at[:, :, pl.ds(at, width)]

    def landing(part, chunk):
        return x_buf.at[part, :, pl.ds(pl.multiple_of(chunk * HALF, HALF), HALF), :]

    @pl.loop(0, parts)
    def _(part):
        for offset in PEERS:
            peer = peer_of(me, offset)
            pltpu.make_async_remote_copy(
                source(peer, part), landing(part, me), x_send.at[part], x_recv.at[part],
                device_id={"tm": peer}, device_id_type=MESH,
            ).start()
        pltpu.make_async_copy(source(me, part), landing(part, me), x_recv.at[part]).start()

    block = lax.broadcasted_iota(jnp.int32, (HALF, 1024), 0)
    chunk = lax.broadcasted_iota(jnp.int32, (HALF, 1024), 1) // HALF
    inside = ((block == chunk) | (block == chunk - 1)) & (block < NB)
    use_even = inside & (block % 2 == 0)
    use_odd = inside & (block % 2 == 1)

    @pl.loop(0, NF)
    def _(j):
        rows = table[order[j]]
        for r in range(2):
            even = jnp.broadcast_to(jnp.tile(rows[r : r + 1], (1, 8)), (HALF, 1024))
            odd = jnp.broadcast_to(jnp.tile(rows[r + 2 : r + 3], (1, 8)), (HALF, 1024))
            band = jnp.where(use_even, even, jnp.where(use_odd, odd, 0.0))
            at = pl.multiple_of(j * NFFT + r * HALF, HALF)
            dft[pl.ds(at, HALF), :] = band.astype(jnp.bfloat16)

    gram[...] = jnp.zeros_like(gram)

    @pl.loop(0, parts)
    def _(part):
        pltpu.make_async_copy(x_buf.at[part], x_buf.at[part], x_recv.at[part]).wait()
        scales = weights[pl.ds(part, 1), :]

        @pl.loop(0, GROUPS)
        def _(g):
            lines = dft[pl.ds(pl.multiple_of(g * GROUP_ROWS, GROUP_ROWS), GROUP_ROWS), :]
            products = gram[g]
            for c in range(COMP):
                found = jnp.dot(lines, x_buf[part, c], preferred_element_type=jnp.float32)
                found = found.astype(jnp.bfloat16)
                spec[g, part, c] = found
                heavy = (found.astype(jnp.float32) * scales).astype(jnp.bfloat16)
                products += lax.dot_general(
                    heavy, found, (((1,), (1,)), ((), ())), preferred_element_type=jnp.float32
                )
            gram[g] = products

    lane = lax.broadcasted_iota(jnp.int32, (HALF, 128), 1)
    low = lane < NFFT
    half_low = low[: HALF // 2]

    @pl.loop(0, GROUPS)
    def _(g):
        for f in range(IN_GROUP):
            tile = gram[g, f * NFFT : (f + 1) * NFFT, (f // 2) * 128 : (f // 2 + 1) * 128]
            if f % 2:
                tile = pltpu.roll(tile, NFFT, 1)
            first, second = tile[:HALF], lane_halves_swapped(tile[HALF:], lane)
            both = first + jnp.where(lane < HALF, second, -second)
            gram_out[g * IN_GROUP + f] = jnp.where(
                half_low, both[: HALF // 2], pltpu.roll(both[HALF // 2 :], NFFT, 1)
            )

    for offset in PEERS:
        peer = peer_of(me, offset)
        pltpu.make_async_remote_copy(
            gram_out.at[peer], gram_in.at[me], g_send, g_recv,
            device_id={"tm": peer}, device_id_type=MESH,
        ).start()
    pltpu.make_async_copy(gram_out.at[me], gram_in.at[me], g_recv).start()
    pltpu.make_async_copy(gram_in, gram_in, g_recv).wait()
    total[row] = jnp.sum(gram_in[...], axis=0)
    for step in range(1, n_space):
        pltpu.make_async_remote_copy(
            total.at[row], total.at[row], y_send, y_recv,
            device_id={"space": lax.rem(row + step, n_space)}, device_id_type=MESH,
        ).start()
    others = total.at[pl.ds(0, n_space - 1)]
    pltpu.make_async_copy(others, others, y_recv).wait()
    packed = total[0]
    for step in range(1, n_space):
        packed = packed + total[step]
    packed = packed * scale

    near = jnp.concatenate([packed, pltpu.roll(packed, NFFT, 1)], axis=0)
    near = jnp.where(low, near, 0.0)
    top = jnp.where(lane < HALF, near, -near)
    bottom = jnp.where(low, lane_halves_swapped(near, lane), 0.0)
    matrix = jnp.concatenate([top, bottom], axis=0)
    empty = jnp.zeros((NFFT, 128), jnp.float32)
    column = lax.broadcasted_iota(jnp.int32, (NFFT, 128), 1)

    def applied(v):
        return jnp.dot(
            matrix, jnp.concatenate([v, empty], axis=0),
            precision=lax.Precision.HIGHEST, preferred_element_type=jnp.float32,
        )

    vec = start[...]
    for _ in range(SWEEPS):
        vec = applied(vec)
        for k in range(MODES):
            new = jnp.broadcast_to(vec[:, k : k + 1], (NFFT, 128))
            new = new / jnp.sqrt(jnp.sum(new * new, axis=0, keepdims=True))
            inner_re = jnp.sum(new * vec, axis=0, keepdims=True)
            inner_im = jnp.sum(new * turned(vec), axis=0, keepdims=True)
            less = vec - (inner_re * new - inner_im * turned(new))
            vec = jnp.where(column == k, new, jnp.where(column > k, less, vec))
    vec = jnp.where(column < MODES, vec, 0.0)

    wide = lax.broadcasted_iota(jnp.int32, (8, 128), 1)
    high = lax.broadcasted_iota(jnp.int32, (8, 128), 0)
    flat = jnp.concatenate([vec * factor, empty], axis=0).T[:8]
    real_rows = jnp.where(wide < HALF, flat, -flat)
    imag_rows = jnp.where(wide < NFFT, lane_halves_swapped(flat, wide), 0.0)
    lines = jnp.where(high < MODES, real_rows, pltpu.roll(imag_rows, MODES, 0))
    place = lax.rem(me, IN_GROUP)
    lines = jnp.where(lax.rem(place, 2) == 1, pltpu.roll(lines, NFFT, 1), lines)
    zero = jnp.zeros_like(lines)
    lines = jnp.concatenate(
        [jnp.where(place < 2, lines, zero), jnp.where(place < 2, zero, lines)], axis=1
    )

    mix[me] = lines
    for offset in PEERS:
        pltpu.make_async_remote_copy(
            mix.at[me], mix.at[me], m_send, m_recv,
            device_id={"tm": peer_of(me, offset)}, device_id_type=MESH,
        ).start()
    energies[...] = jnp.broadcast_to(jnp.sum(vec * applied(vec), axis=0, keepdims=True), (8, 128))
    others = mix.at[pl.ds(0, NF - 1)]
    pltpu.make_async_copy(others, others, m_recv).wait()

    span = pl.ds(pl.multiple_of(me * own, own), own)
    for step in GROUP_ORDER:
        g = lax.rem(me // IN_GROUP + step, GROUPS)
        rows = mix[pl.ds(g * IN_GROUP, IN_GROUP)].reshape(IN_GROUP * 8, GROUP_ROWS)
        rows = rows.astype(jnp.bfloat16)
        for part in range(parts):
            for c in range(COMP):
                made = jnp.dot(rows, spec[g, part, c], preferred_element_type=jnp.float32)
                for f in range(IN_GROUP):
                    out_buf[g * IN_GROUP + f, c, :, part * width : (part + 1) * width] = made[
                        f * 8 : (f + 1) * 8
                    ].astype(jnp.bfloat16)
        for f in range(IN_GROUP):
            j = g * IN_GROUP + f

            @pl.when(j != me)
            def _():
                pltpu.make_async_remote_copy(
                    out_buf.at[j], modes.at[:, :, span], o_send, o_recv,
                    device_id={"tm": j}, device_id_type=MESH,
                ).start()

            @pl.when(j == me)
            def _():
                pltpu.make_async_copy(out_buf.at[j], modes.at[:, :, span], o_recv).start()

    sent = x_buf.at[:, :, pl.ds(0, (NF - 1) * HALF), :]
    for part in range(parts):
        pltpu.make_async_copy(sent.at[part], sent.at[part], x_send.at[part]).wait()
    others = gram_out.at[pl.ds(0, NF - 1)]
    pltpu.make_async_copy(others, others, g_send).wait()
    others = total.at[pl.ds(0, n_space - 1)]
    pltpu.make_async_copy(others, others, y_send).wait()
    others = mix.at[pl.ds(0, NF - 1)]
    pltpu.make_async_copy(others, others, m_send).wait()
    others = out_buf.at[pl.ds(0, NF - 1)]
    pltpu.make_async_copy(others, others, o_send).wait()
    pltpu.make_async_copy(out_buf, out_buf, o_recv).wait()


def per_device(table, energy_sum, snapshots, cell_weights, freq_order):
    n_tm = lax.axis_size("tm")
    cells = snapshots.shape[2]
    own = cells // n_tm
    parts = 4
    width = own // parts
    scale = 1.0 / (energy_sum * COMP * cells * lax.axis_size("space"))
    factor = 1.0 / math.sqrt(energy_sum)
    snaps = jnp.transpose(snapshots, (1, 0, 2))
    weights = lax.dynamic_slice_in_dim(cell_weights, lax.axis_index("tm") * own, own)
    weights = weights.reshape(parts, width)
    dma = pltpu.SemaphoreType.DMA
    vmem = pl.BlockSpec(memory_space=pltpu.VMEM)
    energies, modes = pl.pallas_call(
        functools.partial(kernel, parts, width, scale, factor),
        out_shape=(
            jax.ShapeDtypeStruct((8, 128), jnp.float32),
            jax.ShapeDtypeStruct((COMP, 2 * MODES, cells), jnp.bfloat16),
        ),
        in_specs=[
            pl.BlockSpec(memory_space=pltpu.SMEM),
            pl.BlockSpec(memory_space=pl.ANY),
            vmem,
            vmem,
            vmem,
        ],
        out_specs=(vmem, pl.BlockSpec(memory_space=pl.ANY)),
        scratch_shapes=[
            pltpu.VMEM((parts, COMP, n_tm * HALF, width), jnp.bfloat16),
            pltpu.VMEM((NF * NFFT, n_tm * HALF), jnp.bfloat16),
            pltpu.VMEM((GROUPS, parts, COMP, GROUP_ROWS, width), jnp.bfloat16),
            pltpu.VMEM((GROUPS, GROUP_ROWS, GROUP_ROWS), jnp.float32),
            pltpu.VMEM((NF, HALF // 2, 128), jnp.float32),
            pltpu.VMEM((n_tm, HALF // 2, 128), jnp.float32),
            pltpu.VMEM((lax.axis_size("space"), HALF // 2, 128), jnp.float32),
            pltpu.VMEM((NF, 2 * MODES, GROUP_ROWS), jnp.float32),
            pltpu.VMEM((NF, COMP, 2 * MODES, own), jnp.bfloat16),
            dma((parts,)),
            dma((parts,)),
            dma,
            dma,
            dma,
            dma,
            dma,
            dma,
            dma,
            dma,
        ],
        compiler_params=pltpu.CompilerParams(
            collective_id=0, has_side_effects=True, vmem_limit_bytes=56 << 20
        ),
        name="spod",
    )(freq_order, snaps, weights, table, first_vectors())
    modes = modes.reshape(COMP, 2, MODES, cells).transpose(2, 1, 0, 3)
    return energies[:1, :MODES], modes[None]


def solution(mesh):
    table, energy_sum = basis_rows()
    rounded = table.astype(jnp.bfloat16).astype(np.float32)
    return jax.shard_map(
        functools.partial(per_device, rounded, energy_sum),
        mesh=mesh,
        in_specs=(P("tm", None, "space"), P("space"), P()),
        out_specs=(P("tm", None), P("tm", None, None, None, "space")),
        check_vma=False,
    )
```

```python
import functools
import math

import jax
import jax.numpy as jnp
import numpy as np
from jax import lax
from jax.experimental import pallas as pl
from jax.experimental.pallas import tpu as pltpu
from jax.sharding import PartitionSpec as P

NFFT = 64
COMP = 3
MODES = 4
SWEEPS = 3
HALF = 32
NF = 32
NB = 31
SHIFT = 0.61
MESH = pl.DeviceIdType.MESH

CYCLE = (0, 1, 2, 3)
PEERS = [
    (CYCLE[(turn + lead) % 4], dx, dc)
    for dc in (0, 1)
    for turn in range(4)
    for dx, lead in ((2, 0), (1, 1), (3, 3), (0, 2))
    if (CYCLE[(turn + lead) % 4], dx, dc) != (0, 0, 0)
]
GROUPS = 8
IN_GROUP = NF // GROUPS
GROUP_ROWS = IN_GROUP * 2 * HALF
GROUP_ORDER = (4, 5, 3, 2, 6, 7, 1, 0)
STRIP = 8 * HALF
STRIPS = 4
STEP_ROWS = 8 * NFFT
BAND_ROWS = 9 * NFFT


def peer_of(me, offset):
    z, x, core = me // 8, (me // 2) % 4, me % 2
    return (((z + offset[0]) % 4) * 4 + (x + offset[1]) % 4) * 2 + (core + offset[2]) % 2


def basis_rows():
    sample = np.arange(NFFT)
    freqs = np.arange(NF)
    turn = ((freqs[:, None] * sample[None, :]) % NFFT).astype(np.float32)
    angle = np.float32(2.0 * math.pi) * turn / np.float32(NFFT)
    hann_angle = np.float32(2.0 * math.pi) * sample.astype(np.float32) / np.float32(NFFT)
    hann = np.float32(0.5) - np.float32(0.5) * np.cos(hann_angle)
    basis = np.stack([hann * np.cos(angle), -hann * np.sin(angle)], 1)
    even = np.concatenate([basis, basis], 2)
    odd = np.concatenate([basis[:, :, HALF:], basis, basis[:, :, :HALF]], 2)
    table = np.zeros((NF, 8, 128), np.float32)
    table[:, 0:2] = even
    table[:, 2:4] = odd
    return table, float(np.sum(hann * hann))


def first_vectors():
    rows = np.arange(NB, dtype=np.float32)[:, None] + np.float32(1.0)
    cols = np.arange(MODES, dtype=np.float32)[None, :] + np.float32(1.0)
    table = np.zeros((2 * HALF, 128), np.float32)
    table[:NB, :MODES] = np.cos(np.float32(SHIFT) * rows * cols)
    return table


def turned(y):
    return jnp.concatenate([y[HALF:], -y[:HALF]], axis=0)


def lane_halves_swapped(x, lane):
    return jnp.where(lane < HALF, pltpu.roll(x, 128 - HALF, 1), pltpu.roll(x, HALF, 1))


def kernel(
    parts, width, scale, factor,
    order, snaps, weights, table, start, energies, modes,
    x_buf, w_buf, lines_buf, dft, fresh, spec, gram, gram_out, gram_in, total, mix, out_buf,
    x_send, x_recv, g_send, g_recv, y_send, y_recv, m_send, m_recv, o_send, o_recv, w_sem,
):
    me = lax.axis_index("tm")
    row = lax.axis_index("space")
    n_space = lax.axis_size("space")
    own = parts * width

    barrier = pltpu.get_barrier_semaphore()
    for offset in PEERS:
        pl.semaphore_signal(
            barrier, inc=1, device_id={"tm": peer_of(me, offset)}, device_id_type=MESH
        )
    for step in range(1, n_space):
        pl.semaphore_signal(
            barrier, inc=1, device_id={"space": lax.rem(row + step, n_space)}, device_id_type=MESH
        )
    pl.semaphore_wait(barrier, len(PEERS) + n_space - 1)

    def source(owner, part):
        at = pl.multiple_of(owner * own + part * width, width)
        return snaps.at[:, :, pl.ds(at, width)]

    def landing(part, chunk):
        return x_buf.at[part, :, pl.ds(pl.multiple_of(chunk * HALF, HALF), HALF), :]

    @pl.loop(0, parts)
    def _(part):
        for offset in PEERS:
            peer = peer_of(me, offset)
            pltpu.make_async_remote_copy(
                source(peer, part), landing(part, me), x_send.at[part], x_recv.at[part],
                device_id={"tm": peer}, device_id_type=MESH,
            ).start()
        pltpu.make_async_copy(source(me, part), landing(part, me), x_recv.at[part]).start()

    load = pltpu.make_async_copy(weights.at[me], w_buf, w_sem)
    load.start()
    for j in range(NF):
        rows = table[order[j]]
        lines_buf[0, 2 * j : 2 * j + 2] = rows[0:2]
        lines_buf[1, 2 * j : 2 * j + 2] = rows[2:4]
    time = lax.broadcasted_iota(jnp.int32, (NFFT, STRIP), 1)
    for b in range(9):
        rows = lines_buf[(b - 1) % 2]
        since = time - HALF * (b - 1)
        band = jnp.where((since >= 0) & (since < NFFT), jnp.concatenate([rows, rows], axis=1), 0.0)
        dft[b * NFFT : (b + 1) * NFFT] = band.astype(jnp.bfloat16)

    gram[...] = jnp.zeros_like(gram)
    columns = width // 128
    fresh[:, NB * NFFT :] = jnp.zeros((COMP * columns, NFFT, 128), jnp.float32)
    load.wait()

    @pl.loop(0, parts)
    def _(part):
        pltpu.make_async_copy(x_buf.at[part], x_buf.at[part], x_recv.at[part]).wait()
        scales = jnp.concatenate(
            [w_buf[pl.ds(part * columns + k, 1), :] for k in range(columns)], axis=1
        )
        for c in range(COMP):
            for strip in range(STRIPS):
                first = NFFT if strip == 0 else 0
                last = BAND_ROWS - NFFT if strip == STRIPS - 1 else BAND_ROWS
                made = jnp.dot(
                    dft[first:last], x_buf[part, c, strip * STRIP : (strip + 1) * STRIP],
                    preferred_element_type=jnp.float32,
                )
                at = strip * STEP_ROWS
                for k in range(columns):
                    piece = made[:, k * 128 : (k + 1) * 128]
                    if strip:
                        fresh[c * columns + k, at - NFFT : at] += piece[:NFFT]
                        piece = piece[NFFT:]
                    fresh[c * columns + k, at : at + piece.shape[0]] = piece

        @pl.loop(0, GROUPS)
        def _(g):
            products = gram[g]
            for c in range(COMP):
                found = jnp.concatenate(
                    [
                        jnp.concatenate(
                            [
                                fresh[c * columns + k, pl.ds(g * 8 + line, HALF, stride=NFFT), :]
                                for line in range(8)
                            ],
                            axis=0,
                        )
                        for k in range(columns)
                    ],
                    axis=1,
                ).astype(jnp.bfloat16)
                spec[g, part, c] = found
                heavy = (found.astype(jnp.float32) * scales).astype(jnp.bfloat16)
                products += lax.dot_general(
                    heavy, found, (((1,), (1,)), ((), ())), preferred_element_type=jnp.float32
                )
            gram[g] = products

    lane = lax.broadcasted_iota(jnp.int32, (HALF, 128), 1)
    low = lane < NFFT
    half_low = low[: HALF // 2]

    @pl.loop(0, GROUPS)
    def _(g):
        for f in range(IN_GROUP):
            tile = gram[g, f * NFFT : (f + 1) * NFFT, (f // 2) * 128 : (f // 2 + 1) * 128]
            if f % 2:
                tile = pltpu.roll(tile, NFFT, 1)
            first, second = tile[:HALF], lane_halves_swapped(tile[HALF:], lane)
            both = first + jnp.where(lane < HALF, second, -second)
            gram_out[g * IN_GROUP + f] = jnp.where(
                half_low, both[: HALF // 2], pltpu.roll(both[HALF // 2 :], NFFT, 1)
            )

    for offset in PEERS:
        peer = peer_of(me, offset)
        pltpu.make_async_remote_copy(
            gram_out.at[peer], gram_in.at[me], g_send, g_recv,
            device_id={"tm": peer}, device_id_type=MESH,
        ).start()
    pltpu.make_async_copy(gram_out.at[me], gram_in.at[me], g_recv).start()
    pltpu.make_async_copy(gram_in, gram_in, g_recv).wait()
    total[row] = jnp.sum(gram_in[...], axis=0)
    for step in range(1, n_space):
        pltpu.make_async_remote_copy(
            total.at[row], total.at[row], y_send, y_recv,
            device_id={"space": lax.rem(row + step, n_space)}, device_id_type=MESH,
        ).start()
    others = total.at[pl.ds(0, n_space - 1)]
    pltpu.make_async_copy(others, others, y_recv).wait()
    packed = total[0]
    for step in range(1, n_space):
        packed = packed + total[step]
    packed = packed * scale

    near = jnp.concatenate([packed, pltpu.roll(packed, NFFT, 1)], axis=0)
    near = jnp.where(low, near, 0.0)
    top = jnp.where(lane < HALF, near, -near)
    bottom = jnp.where(low, lane_halves_swapped(near, lane), 0.0)
    matrix = jnp.concatenate([top, bottom], axis=0)
    empty = jnp.zeros((NFFT, 128), jnp.float32)
    column = lax.broadcasted_iota(jnp.int32, (NFFT, 128), 1)

    def applied(v):
        return jnp.dot(
            matrix, jnp.concatenate([v, empty], axis=0),
            precision=lax.Precision.HIGHEST, preferred_element_type=jnp.float32,
        )

    vec = start[...]
    for _ in range(SWEEPS):
        vec = applied(vec)
        for k in range(MODES):
            new = jnp.broadcast_to(vec[:, k : k + 1], (NFFT, 128))
            new = new / jnp.sqrt(jnp.sum(new * new, axis=0, keepdims=True))
            inner_re = jnp.sum(new * vec, axis=0, keepdims=True)
            inner_im = jnp.sum(new * turned(vec), axis=0, keepdims=True)
            less = vec - (inner_re * new - inner_im * turned(new))
            vec = jnp.where(column == k, new, jnp.where(column > k, less, vec))
    vec = jnp.where(column < MODES, vec, 0.0)

    wide = lax.broadcasted_iota(jnp.int32, (8, 128), 1)
    flat = jnp.concatenate([vec * factor, empty], axis=0).T[:8]
    real_rows = jnp.where(wide < HALF, flat, -flat)
    imag_rows = jnp.where(wide < NFFT, lane_halves_swapped(flat, wide), 0.0)
    lines = jnp.concatenate(
        [rows[k : k + 1] for k in range(MODES) for rows in (real_rows, imag_rows)], axis=0
    )
    lines = jnp.where(lax.rem(me, 2) == 1, pltpu.roll(lines, NFFT, 1), lines)

    mix[me] = lines.astype(jnp.bfloat16)
    for offset in PEERS:
        pltpu.make_async_remote_copy(
            mix.at[me], mix.at[me], m_send, m_recv,
            device_id={"tm": peer_of(me, offset)}, device_id_type=MESH,
        ).start()
    energies[...] = jnp.sum(vec * applied(vec), axis=0, keepdims=True)[:, :MODES]
    others = mix.at[pl.ds(0, NF - 1)]
    pltpu.make_async_copy(others, others, m_recv).wait()

    span = pl.ds(pl.multiple_of(me * own, own), own)
    for step in GROUP_ORDER:
        g = lax.rem(me // IN_GROUP + step, GROUPS)
        zero = jnp.zeros((8, 128), jnp.float32)
        rows = [mix[g * IN_GROUP + f].astype(jnp.float32) for f in range(IN_GROUP)]
        rows = [
            jnp.concatenate([line, zero] if f < 2 else [zero, line], axis=1)
            for f, line in enumerate(rows)
        ]
        rows = jnp.concatenate(rows, axis=0).astype(jnp.bfloat16)
        for part in range(parts):
            for c in range(COMP):
                made = jnp.dot(rows, spec[g, part, c], preferred_element_type=jnp.float32)
                made = made.astype(jnp.bfloat16)
                here = slice(part * width, (part + 1) * width)
                for f in range(IN_GROUP):
                    for k in range(MODES):
                        out_buf[g * IN_GROUP + f, k * COMP + c, :, here] = made[
                            f * 8 + 2 * k : f * 8 + 2 * k + 2
                        ]
        for f in range(IN_GROUP):
            j = g * IN_GROUP + f

            @pl.when(j != me)
            def _():
                pltpu.make_async_remote_copy(
                    out_buf.at[j], modes.at[:, :, span], o_send, o_recv,
                    device_id={"tm": j}, device_id_type=MESH,
                ).start()

            @pl.when(j == me)
            def _():
                pltpu.make_async_copy(out_buf.at[j], modes.at[:, :, span], o_recv).start()

    sent = x_buf.at[:, :, pl.ds(0, (NF - 1) * HALF), :]
    for part in range(parts):
        pltpu.make_async_copy(sent.at[part], sent.at[part], x_send.at[part]).wait()
    others = gram_out.at[pl.ds(0, NF - 1)]
    pltpu.make_async_copy(others, others, g_send).wait()
    others = total.at[pl.ds(0, n_space - 1)]
    pltpu.make_async_copy(others, others, y_send).wait()
    others = mix.at[pl.ds(0, NF - 1)]
    pltpu.make_async_copy(others, others, m_send).wait()
    others = out_buf.at[pl.ds(0, NF - 1)]
    pltpu.make_async_copy(others, others, o_send).wait()
    pltpu.make_async_copy(out_buf, out_buf, o_recv).wait()


def per_device(table, energy_sum, snapshots, cell_weights, freq_order):
    n_tm = lax.axis_size("tm")
    cells = snapshots.shape[2]
    own = cells // n_tm
    parts = 4
    width = own // parts
    scale = 1.0 / (energy_sum * COMP * cells * lax.axis_size("space"))
    factor = 1.0 / math.sqrt(energy_sum)
    snaps = jnp.transpose(snapshots, (1, 0, 2))
    weights = cell_weights.reshape(n_tm, own // 128, 128)
    dma = pltpu.SemaphoreType.DMA
    vmem = pl.BlockSpec(memory_space=pltpu.VMEM)
    energies, modes = pl.pallas_call(
        functools.partial(kernel, parts, width, scale, factor),
        out_shape=(
            jax.ShapeDtypeStruct((1, MODES), jnp.float32),
            jax.ShapeDtypeStruct((MODES * COMP, 2, cells), jnp.bfloat16),
        ),
        in_specs=[
            pl.BlockSpec(memory_space=pltpu.SMEM),
            pl.BlockSpec(memory_space=pl.ANY),
            pl.BlockSpec(memory_space=pl.ANY),
            vmem,
            vmem,
        ],
        out_specs=(vmem, pl.BlockSpec(memory_space=pl.ANY)),
        scratch_shapes=[
            pltpu.VMEM((parts, COMP, n_tm * HALF, width), jnp.bfloat16),
            pltpu.VMEM((own // 128, 128), jnp.float32),
            pltpu.VMEM((2, NFFT, 128), jnp.float32),
            pltpu.VMEM((BAND_ROWS, STRIP), jnp.bfloat16),
            pltpu.VMEM((COMP * width // 128, NF * NFFT, 128), jnp.float32),
            pltpu.VMEM((GROUPS, parts, COMP, GROUP_ROWS, width), jnp.bfloat16),
            pltpu.VMEM((GROUPS, GROUP_ROWS, GROUP_ROWS), jnp.float32),
            pltpu.VMEM((NF, HALF // 2, 128), jnp.float32),
            pltpu.VMEM((n_tm, HALF // 2, 128), jnp.float32),
            pltpu.VMEM((lax.axis_size("space"), HALF // 2, 128), jnp.float32),
            pltpu.VMEM((NF, 2 * MODES, 128), jnp.bfloat16),
            pltpu.VMEM((NF, MODES * COMP, 2, own), jnp.bfloat16),
            dma((parts,)),
            dma((parts,)),
            dma,
            dma,
            dma,
            dma,
            dma,
            dma,
            dma,
            dma,
            dma,
        ],
        compiler_params=pltpu.CompilerParams(
            collective_id=0, has_side_effects=True, vmem_limit_bytes=56 << 20
        ),
        name="spod",
    )(freq_order, snaps, weights, table, first_vectors())
    modes = modes.reshape(MODES, COMP, 2, cells).transpose(0, 2, 1, 3)
    return energies, modes[None]


def solution(mesh):
    table, energy_sum = basis_rows()
    rounded = table.astype(jnp.bfloat16).astype(np.float32)
    return jax.shard_map(
        functools.partial(per_device, rounded, energy_sum),
        mesh=mesh,
        in_specs=(P("tm", None, "space"), P("space"), P()),
        out_specs=(P("tm", None), P("tm", None, None, None, "space")),
        check_vma=False,
    )
```

```python
import functools
import math

import jax
import jax.numpy as jnp
import numpy as np
from jax import lax
from jax.experimental import pallas as pl
from jax.experimental.pallas import tpu as pltpu
from jax.sharding import PartitionSpec as P

NFFT = 64
COMP = 3
MODES = 4
SWEEPS = 3
HALF = 32
NF = 32
NB = 31
SHIFT = 0.61
MESH = pl.DeviceIdType.MESH

CYCLE = (0, 1, 2, 3)
PEERS = [
    (CYCLE[(turn + lead) % 4], dx, dc)
    for dc in (0, 1)
    for turn in range(4)
    for dx, lead in ((2, 0), (1, 1), (3, 3), (0, 2))
    if (CYCLE[(turn + lead) % 4], dx, dc) != (0, 0, 0)
]
GROUPS = 8
IN_GROUP = NF // GROUPS
GROUP_ROWS = IN_GROUP * 2 * HALF
GROUP_ORDER = (4, 5, 3, 2, 6, 7, 1, 0)
STRIP = 8 * HALF
STRIPS = 4
STRIP_ROWS = 8 * 2 * NF


def peer_of(me, offset):
    z, x, core = me // 8, (me // 2) % 4, me % 2
    return (((z + offset[0]) % 4) * 4 + (x + offset[1]) % 4) * 2 + (core + offset[2]) % 2


def basis_rows():
    sample = np.arange(NFFT)
    freqs = np.arange(NF)
    turn = ((freqs[:, None] * sample[None, :]) % NFFT).astype(np.float32)
    angle = np.float32(2.0 * math.pi) * turn / np.float32(NFFT)
    hann_angle = np.float32(2.0 * math.pi) * sample.astype(np.float32) / np.float32(NFFT)
    hann = np.float32(0.5) - np.float32(0.5) * np.cos(hann_angle)
    basis = np.stack([hann * np.cos(angle), -hann * np.sin(angle)], 1)
    even = np.concatenate([basis, basis], 2)
    odd = np.concatenate([basis[:, :, HALF:], basis, basis[:, :, :HALF]], 2)
    table = np.zeros((NF, 8, 128), np.float32)
    table[:, 0:2] = even
    table[:, 2:4] = odd
    return table, float(np.sum(hann * hann))


def first_vectors():
    rows = np.arange(NB, dtype=np.float32)[:, None] + np.float32(1.0)
    cols = np.arange(MODES, dtype=np.float32)[None, :] + np.float32(1.0)
    table = np.zeros((2 * HALF, 128), np.float32)
    table[:NB, :MODES] = np.cos(np.float32(SHIFT) * rows * cols)
    return table


def turned(y):
    return jnp.concatenate([y[HALF:], -y[:HALF]], axis=0)


def lane_halves_swapped(x, lane):
    return jnp.where(lane < HALF, pltpu.roll(x, 128 - HALF, 1), pltpu.roll(x, HALF, 1))


def kernel(
    parts, width, scale, factor,
    order, snaps, weights, table, start, energies, modes,
    x_buf, w_buf, dft, dft_end, fresh, spec, gram, gram_out, gram_in, total, mix, out_buf,
    x_send, x_recv, g_send, g_recv, y_send, y_recv, m_send, m_recv, o_send, o_recv, w_sem,
):
    me = lax.axis_index("tm")
    row = lax.axis_index("space")
    n_space = lax.axis_size("space")
    own = parts * width

    barrier = pltpu.get_barrier_semaphore()
    for offset in PEERS:
        pl.semaphore_signal(
            barrier, inc=1, device_id={"tm": peer_of(me, offset)}, device_id_type=MESH
        )
    for step in range(1, n_space):
        pl.semaphore_signal(
            barrier, inc=1, device_id={"space": lax.rem(row + step, n_space)}, device_id_type=MESH
        )
    pl.semaphore_wait(barrier, len(PEERS) + n_space - 1)

    def source(owner, part):
        at = pl.multiple_of(owner * own + part * width, width)
        return snaps.at[:, :, pl.ds(at, width)]

    def landing(part, chunk):
        return x_buf.at[part, :, pl.ds(pl.multiple_of(chunk * HALF, HALF), HALF), :]

    @pl.loop(0, parts)
    def _(part):
        for offset in PEERS:
            peer = peer_of(me, offset)
            pltpu.make_async_remote_copy(
                source(peer, part), landing(part, me), x_send.at[part], x_recv.at[part],
                device_id={"tm": peer}, device_id_type=MESH,
            ).start()
        pltpu.make_async_copy(source(me, part), landing(part, me), x_recv.at[part]).start()

    load = pltpu.make_async_copy(weights.at[me], w_buf, w_sem)
    load.start()
    block = lax.broadcasted_iota(jnp.int32, (8, 2 * STRIP), 0)
    since = lax.broadcasted_iota(jnp.int32, (8, 2 * STRIP), 1) - HALF * block
    inside = (since >= 0) & (since < NFFT)
    use_even = inside & (block % 2 == 0)
    use_odd = inside & (block % 2 == 1)
    present = (block < 7)[:, :STRIP]

    @pl.loop(0, NF)
    def _(j):
        rows = table[order[j]]
        bands = []
        for r in range(2):
            even = jnp.broadcast_to(jnp.tile(rows[r : r + 1], (1, 4)), (8, 2 * STRIP))
            odd = jnp.broadcast_to(jnp.tile(rows[r + 2 : r + 3], (1, 4)), (8, 2 * STRIP))
            bands.append(jnp.where(use_even, even, jnp.where(use_odd, odd, 0.0)))
        at = pl.ds(pl.multiple_of(j * 16, 16), 16)
        dft[at, :] = jnp.concatenate(bands, axis=0).astype(jnp.bfloat16)
        bands = [jnp.where(present, band[:, :STRIP], 0.0) for band in bands]
        dft_end[at, :] = jnp.concatenate(bands, axis=0).astype(jnp.bfloat16)

    gram[...] = jnp.zeros_like(gram)
    columns = width // 128
    load.wait()

    @pl.loop(0, parts)
    def _(part):
        pltpu.make_async_copy(x_buf.at[part], x_buf.at[part], x_recv.at[part]).wait()
        scales = jnp.concatenate(
            [w_buf[pl.ds(part * columns + k, 1), :] for k in range(columns)], axis=1
        )
        for c in range(COMP):
            for strip in range(STRIPS):
                last = strip == STRIPS - 1
                rows = slice(strip * STRIP, (strip + 1 if last else strip + 2) * STRIP)
                fresh[c, strip] = jnp.dot(
                    (dft_end if last else dft)[...], x_buf[part, c, rows],
                    preferred_element_type=jnp.float32,
                )

        @pl.loop(0, GROUPS)
        def _(g):
            products = gram[g]
            for c in range(COMP):
                pieces = [
                    fresh[c, strip, pl.ds(pl.multiple_of(g * 64, 64), 64), :]
                    for strip in range(STRIPS)
                ]
                found = jnp.concatenate(
                    [piece[line * 8 : line * 8 + 8] for line in range(8) for piece in pieces],
                    axis=0,
                ).astype(jnp.bfloat16)
                spec[g, part, c] = found
                heavy = (found.astype(jnp.float32) * scales).astype(jnp.bfloat16)
                products += lax.dot_general(
                    heavy, found, (((1,), (1,)), ((), ())), preferred_element_type=jnp.float32
                )
            gram[g] = products

    lane = lax.broadcasted_iota(jnp.int32, (HALF, 128), 1)
    low = lane < NFFT
    half_low = low[: HALF // 2]

    @pl.loop(0, GROUPS)
    def _(g):
        for f in range(IN_GROUP):
            tile = gram[g, f * NFFT : (f + 1) * NFFT, (f // 2) * 128 : (f // 2 + 1) * 128]
            if f % 2:
                tile = pltpu.roll(tile, NFFT, 1)
            first, second = tile[:HALF], lane_halves_swapped(tile[HALF:], lane)
            both = first + jnp.where(lane < HALF, second, -second)
            gram_out[g * IN_GROUP + f] = jnp.where(
                half_low, both[: HALF // 2], pltpu.roll(both[HALF // 2 :], NFFT, 1)
            )

    for offset in PEERS:
        peer = peer_of(me, offset)
        pltpu.make_async_remote_copy(
            gram_out.at[peer], gram_in.at[me], g_send, g_recv,
            device_id={"tm": peer}, device_id_type=MESH,
        ).start()
    pltpu.make_async_copy(gram_out.at[me], gram_in.at[me], g_recv).start()
    pltpu.make_async_copy(gram_in, gram_in, g_recv).wait()
    total[row] = jnp.sum(gram_in[...], axis=0)
    for step in range(1, n_space):
        pltpu.make_async_remote_copy(
            total.at[row], total.at[row], y_send, y_recv,
            device_id={"space": lax.rem(row + step, n_space)}, device_id_type=MESH,
        ).start()
    others = total.at[pl.ds(0, n_space - 1)]
    pltpu.make_async_copy(others, others, y_recv).wait()
    packed = total[0]
    for step in range(1, n_space):
        packed = packed + total[step]
    packed = packed * scale

    near = jnp.concatenate([packed, pltpu.roll(packed, NFFT, 1)], axis=0)
    near = jnp.where(low, near, 0.0)
    top = jnp.where(lane < HALF, near, -near)
    bottom = jnp.where(low, lane_halves_swapped(near, lane), 0.0)
    matrix = jnp.concatenate([top, bottom], axis=0)
    empty = jnp.zeros((NFFT, 128), jnp.float32)
    column = lax.broadcasted_iota(jnp.int32, (NFFT, 128), 1)

    def applied(v):
        return jnp.dot(
            matrix, jnp.concatenate([v, empty], axis=0),
            precision=lax.Precision.HIGHEST, preferred_element_type=jnp.float32,
        )

    vec = start[...]
    for _ in range(SWEEPS):
        vec = applied(vec)
        for k in range(MODES):
            new = jnp.broadcast_to(vec[:, k : k + 1], (NFFT, 128))
            new = new / jnp.sqrt(jnp.sum(new * new, axis=0, keepdims=True))
            inner_re = jnp.sum(new * vec, axis=0, keepdims=True)
            inner_im = jnp.sum(new * turned(vec), axis=0, keepdims=True)
            less = vec - (inner_re * new - inner_im * turned(new))
            vec = jnp.where(column == k, new, jnp.where(column > k, less, vec))
    vec = jnp.where(column < MODES, vec, 0.0)

    wide = lax.broadcasted_iota(jnp.int32, (8, 128), 1)
    flat = jnp.concatenate([vec * factor, empty], axis=0).T[:8]
    real_rows = jnp.where(wide < HALF, flat, -flat)
    imag_rows = jnp.where(wide < NFFT, lane_halves_swapped(flat, wide), 0.0)
    lines = jnp.concatenate(
        [rows[k : k + 1] for k in range(MODES) for rows in (real_rows, imag_rows)], axis=0
    )
    lines = jnp.where(lax.rem(me, 2) == 1, pltpu.roll(lines, NFFT, 1), lines)

    mix[me] = lines.astype(jnp.bfloat16)
    for offset in PEERS:
        pltpu.make_async_remote_copy(
            mix.at[me], mix.at[me], m_send, m_recv,
            device_id={"tm": peer_of(me, offset)}, device_id_type=MESH,
        ).start()
    energies[...] = jnp.sum(vec * applied(vec), axis=0, keepdims=True)[:, :MODES]
    others = mix.at[pl.ds(0, NF - 1)]
    pltpu.make_async_copy(others, others, m_recv).wait()

    span = pl.ds(pl.multiple_of(me * own, own), own)
    for step in GROUP_ORDER:
        g = lax.rem(me // IN_GROUP + step, GROUPS)
        zero = jnp.zeros((8, 128), jnp.float32)
        rows = [mix[g * IN_GROUP + f].astype(jnp.float32) for f in range(IN_GROUP)]
        rows = [
            jnp.concatenate([line, zero] if f < 2 else [zero, line], axis=1)
            for f, line in enumerate(rows)
        ]
        rows = jnp.concatenate(rows, axis=0).astype(jnp.bfloat16)
        for part in range(parts):
            for c in range(COMP):
                made = jnp.dot(rows, spec[g, part, c], preferred_element_type=jnp.float32)
                made = made.astype(jnp.bfloat16)
                here = slice(part * width, (part + 1) * width)
                for f in range(IN_GROUP):
                    for k in range(MODES):
                        out_buf[g * IN_GROUP + f, k * COMP + c, :, here] = made[
                            f * 8 + 2 * k : f * 8 + 2 * k + 2
                        ]
        for f in range(IN_GROUP):
            j = g * IN_GROUP + f

            @pl.when(j != me)
            def _():
                pltpu.make_async_remote_copy(
                    out_buf.at[j], modes.at[:, :, span], o_send, o_recv,
                    device_id={"tm": j}, device_id_type=MESH,
                ).start()

            @pl.when(j == me)
            def _():
                pltpu.make_async_copy(out_buf.at[j], modes.at[:, :, span], o_recv).start()

    sent = x_buf.at[:, :, pl.ds(0, (NF - 1) * HALF), :]
    for part in range(parts):
        pltpu.make_async_copy(sent.at[part], sent.at[part], x_send.at[part]).wait()
    others = gram_out.at[pl.ds(0, NF - 1)]
    pltpu.make_async_copy(others, others, g_send).wait()
    others = total.at[pl.ds(0, n_space - 1)]
    pltpu.make_async_copy(others, others, y_send).wait()
    others = mix.at[pl.ds(0, NF - 1)]
    pltpu.make_async_copy(others, others, m_send).wait()
    others = out_buf.at[pl.ds(0, NF - 1)]
    pltpu.make_async_copy(others, others, o_send).wait()
    pltpu.make_async_copy(out_buf, out_buf, o_recv).wait()


def hand_over(energies, modes, energies_out, modes_out, held, in_sem, out_sem):
    energies_out[...] = energies[...]
    rows = range(modes.shape[0])
    takes = [pltpu.make_async_copy(modes.at[k], held.at[k], in_sem.at[k]) for k in rows]
    gives = [pltpu.make_async_copy(held.at[k], modes_out.at[k], out_sem.at[k]) for k in rows]
    for take in takes:
        take.start()
    for take, give in zip(takes, gives):
        take.wait()
        give.start()
    for give in gives:
        give.wait()


def per_device(table, energy_sum, snapshots, cell_weights, freq_order):
    n_tm = lax.axis_size("tm")
    cells = snapshots.shape[2]
    own = cells // n_tm
    parts = 4
    width = own // parts
    scale = 1.0 / (energy_sum * COMP * cells * lax.axis_size("space"))
    factor = 1.0 / math.sqrt(energy_sum)
    snaps = jnp.transpose(snapshots, (1, 0, 2))
    weights = cell_weights.reshape(n_tm, own // 128, 128)
    dma = pltpu.SemaphoreType.DMA
    vmem = pl.BlockSpec(memory_space=pltpu.VMEM)
    energies, modes = pl.pallas_call(
        functools.partial(kernel, parts, width, scale, factor),
        out_shape=(
            jax.ShapeDtypeStruct((1, MODES), jnp.float32),
            jax.ShapeDtypeStruct((MODES * COMP, 2, cells), jnp.bfloat16),
        ),
        in_specs=[
            pl.BlockSpec(memory_space=pltpu.SMEM),
            pl.BlockSpec(memory_space=pl.ANY),
            pl.BlockSpec(memory_space=pl.ANY),
            vmem,
            vmem,
        ],
        out_specs=(vmem, pl.BlockSpec(memory_space=pl.ANY)),
        scratch_shapes=[
            pltpu.VMEM((parts, COMP, n_tm * HALF, width), jnp.bfloat16),
            pltpu.VMEM((own // 128, 128), jnp.float32),
            pltpu.VMEM((STRIP_ROWS, 2 * STRIP), jnp.bfloat16),
            pltpu.VMEM((STRIP_ROWS, STRIP), jnp.bfloat16),
            pltpu.VMEM((COMP, STRIPS, STRIP_ROWS, width), jnp.float32),
            pltpu.VMEM((GROUPS, parts, COMP, GROUP_ROWS, width), jnp.bfloat16),
            pltpu.VMEM((GROUPS, GROUP_ROWS, GROUP_ROWS), jnp.float32),
            pltpu.VMEM((NF, HALF // 2, 128), jnp.float32),
            pltpu.VMEM((n_tm, HALF // 2, 128), jnp.float32),
            pltpu.VMEM((lax.axis_size("space"), HALF // 2, 128), jnp.float32),
            pltpu.VMEM((NF, 2 * MODES, 128), jnp.bfloat16),
            pltpu.VMEM((NF, MODES * COMP, 2, own), jnp.bfloat16),
            dma((parts,)),
            dma((parts,)),
            dma,
            dma,
            dma,
            dma,
            dma,
            dma,
            dma,
            dma,
            dma,
        ],
        compiler_params=pltpu.CompilerParams(
            collective_id=0, has_side_effects=True, vmem_limit_bytes=56 << 20
        ),
        name="spod",
    )(freq_order, snaps, weights, table, first_vectors())
    energies, modes = pl.pallas_call(
        hand_over,
        out_shape=(
            jax.ShapeDtypeStruct(energies.shape, energies.dtype),
            jax.ShapeDtypeStruct(modes.shape, modes.dtype),
        ),
        in_specs=[vmem, pl.BlockSpec(memory_space=pl.ANY)],
        out_specs=(vmem, pl.BlockSpec(memory_space=pl.ANY)),
        scratch_shapes=[
            pltpu.VMEM(modes.shape, modes.dtype),
            dma((MODES * COMP,)),
            dma((MODES * COMP,)),
        ],
        name="hand_over",
    )(energies, modes)
    modes = modes.reshape(MODES, COMP, 2, cells).transpose(0, 2, 1, 3)
    return energies, modes[None]


def solution(mesh):
    table, energy_sum = basis_rows()
    rounded = table.astype(jnp.bfloat16).astype(np.float32)
    return jax.shard_map(
        functools.partial(per_device, rounded, energy_sum),
        mesh=mesh,
        in_specs=(P("tm", None, "space"), P("space"), P()),
        out_specs=(P("tm", None), P("tm", None, None, None, "space")),
        check_vma=False,
    )
```

```python
import functools
import math

import jax
import jax.numpy as jnp
import numpy as np
from jax import lax
from jax.experimental import pallas as pl
from jax.experimental.pallas import tpu as pltpu
from jax.sharding import PartitionSpec as P

NFFT = 64
COMP = 3
MODES = 4
SWEEPS = 3
HALF = 32
NF = 32
NB = 31
SHIFT = 0.61
MESH = pl.DeviceIdType.MESH

CYCLE = (0, 1, 2, 3)
PEERS = [
    (CYCLE[(turn + lead) % 4], dx, dc)
    for dc in (0, 1)
    for turn in range(4)
    for dx, lead in ((2, 0), (1, 1), (3, 3), (0, 2))
    if (CYCLE[(turn + lead) % 4], dx, dc) != (0, 0, 0)
]
GROUPS = 8
IN_GROUP = NF // GROUPS
GROUP_ROWS = IN_GROUP * 2 * HALF
GROUP_ORDER = (0, 1, 5, 2, 6, 4, 3, 7)
STRIP = 8 * HALF
STRIPS = 4
STRIP_ROWS = 8 * 2 * NF


def peer_of(me, offset):
    z, x, core = me // 8, (me // 2) % 4, me % 2
    return (((z + offset[0]) % 4) * 4 + (x + offset[1]) % 4) * 2 + (core + offset[2]) % 2


def basis_rows():
    sample = np.arange(NFFT)
    freqs = np.arange(NF)
    turn = ((freqs[:, None] * sample[None, :]) % NFFT).astype(np.float32)
    angle = np.float32(2.0 * math.pi) * turn / np.float32(NFFT)
    hann_angle = np.float32(2.0 * math.pi) * sample.astype(np.float32) / np.float32(NFFT)
    hann = np.float32(0.5) - np.float32(0.5) * np.cos(hann_angle)
    basis = np.stack([hann * np.cos(angle), -hann * np.sin(angle)], 1)
    even = np.concatenate([basis, basis], 2)
    odd = np.concatenate([basis[:, :, HALF:], basis, basis[:, :, :HALF]], 2)
    table = np.zeros((NF, 8, 128), np.float32)
    table[:, 0:2] = even
    table[:, 2:4] = odd
    return table, float(np.sum(hann * hann))


def first_vectors():
    rows = np.arange(NB, dtype=np.float32)[:, None] + np.float32(1.0)
    cols = np.arange(MODES, dtype=np.float32)[None, :] + np.float32(1.0)
    table = np.zeros((2 * HALF, 128), np.float32)
    table[:NB, :MODES] = np.cos(np.float32(SHIFT) * rows * cols)
    return table


def turned(y):
    return jnp.concatenate([y[HALF:], -y[:HALF]], axis=0)


def lane_halves_swapped(x, lane):
    return jnp.where(lane < HALF, pltpu.roll(x, 128 - HALF, 1), pltpu.roll(x, HALF, 1))


def kernel(
    parts, width, scale, factor,
    order_far, snaps, weights, table_far, start_far, energies, modes,
    order, table, start, w_buf, x_buf, dft, dft_end, fresh, spec, gram,
    gram_out, gram_in, total, mine, mix, out_buf,
    load_sem, x_send, x_recv, g_send, g_recv, y_send, y_recv, m_send, m_recv, o_send, o_recv,
):
    me = lax.axis_index("tm")
    row = lax.axis_index("space")
    n_space = lax.axis_size("space")
    own = parts * width
    last_part = parts - 1
    home = me // IN_GROUP

    barrier = pltpu.get_barrier_semaphore()
    for offset in PEERS:
        pl.semaphore_signal(
            barrier, inc=1, device_id={"tm": peer_of(me, offset)}, device_id_type=MESH
        )
    for step in range(1, n_space):
        pl.semaphore_signal(
            barrier, inc=1, device_id={"space": lax.rem(row + step, n_space)}, device_id_type=MESH
        )
    loads = [
        pltpu.make_async_copy(far, near, load_sem.at[k])
        for k, (far, near) in enumerate(
            ((order_far, order), (table_far, table), (start_far, start), (weights.at[me], w_buf))
        )
    ]
    for load in loads:
        load.start()
    pl.semaphore_wait(barrier, len(PEERS) + n_space - 1)

    def source(owner, part):
        at = pl.multiple_of(owner * own + part * width, width)
        return snaps.at[:, :, pl.ds(at, width)]

    def landing(part, chunk):
        return x_buf.at[part, :, pl.ds(pl.multiple_of(chunk * HALF, HALF), HALF), :]

    @pl.loop(0, parts)
    def _(part):
        for offset in PEERS:
            peer = peer_of(me, offset)
            pltpu.make_async_remote_copy(
                source(peer, part), landing(part, me), x_send.at[part], x_recv.at[part],
                device_id={"tm": peer}, device_id_type=MESH,
            ).start()
        pltpu.make_async_copy(source(me, part), landing(part, me), x_recv.at[part]).start()

    block = lax.broadcasted_iota(jnp.int32, (8, 2 * STRIP), 0)
    since = lax.broadcasted_iota(jnp.int32, (8, 2 * STRIP), 1) - HALF * block
    inside = (since >= 0) & (since < NFFT)
    use_even = inside & (block % 2 == 0)
    use_odd = inside & (block % 2 == 1)
    present = (block < 7)[:, :STRIP]
    for load in loads:
        load.wait()

    @pl.loop(0, NF)
    def _(j):
        rows = table[order[j]]
        bands = []
        for r in range(2):
            even = jnp.broadcast_to(jnp.tile(rows[r : r + 1], (1, 4)), (8, 2 * STRIP))
            odd = jnp.broadcast_to(jnp.tile(rows[r + 2 : r + 3], (1, 4)), (8, 2 * STRIP))
            bands.append(jnp.where(use_even, even, jnp.where(use_odd, odd, 0.0)))
        at = pl.ds(pl.multiple_of(j * 16, 16), 16)
        dft[at, :] = jnp.concatenate(bands, axis=0).astype(jnp.bfloat16)
        bands = [jnp.where(present, band[:, :STRIP], 0.0) for band in bands]
        dft_end[at, :] = jnp.concatenate(bands, axis=0).astype(jnp.bfloat16)

    gram[...] = jnp.zeros_like(gram)

    def transform(part):
        pltpu.make_async_copy(x_buf.at[part], x_buf.at[part], x_recv.at[part]).wait()
        for strip in range(STRIPS):
            last = strip == STRIPS - 1
            rows = slice(strip * STRIP, (strip + 1 if last else strip + 2) * STRIP)
            given = jnp.concatenate([x_buf[part, c, rows] for c in range(COMP)], axis=1)
            fresh[strip] = jnp.dot(
                (dft_end if last else dft)[...], given, preferred_element_type=jnp.float32
            )

    def accumulate(part, g):
        pieces = [fresh[k, pl.ds(pl.multiple_of(g * 64, 64), 64), :] for k in range(STRIPS)]
        found = jnp.concatenate(
            [piece[line * 8 : line * 8 + 8] for line in range(8) for piece in pieces], axis=0
        ).astype(jnp.bfloat16)
        spec[g, part] = found
        scales = jnp.tile(w_buf[pl.ds(part, 1), :], (1, COMP))
        heavy = (found.astype(jnp.float32) * scales).astype(jnp.bfloat16)
        gram[g] += lax.dot_general(
            heavy, found, (((1,), (1,)), ((), ())), preferred_element_type=jnp.float32
        )

    @pl.loop(0, last_part)
    def _(part):
        transform(part)

        @pl.loop(0, GROUPS)
        def _(g):
            accumulate(part, g)

    lane = lax.broadcasted_iota(jnp.int32, (HALF, 128), 1)
    low = lane < NFFT
    half_low = low[: HALF // 2]
    transform(last_part)

    @pl.loop(0, GROUPS)
    def _(step):
        g = lax.rem(home + step, GROUPS)
        accumulate(last_part, g)
        for f in range(IN_GROUP):
            j = g * IN_GROUP + f
            tile = gram[g, f * NFFT : (f + 1) * NFFT, (f // 2) * 128 : (f // 2 + 1) * 128]
            if f % 2:
                tile = pltpu.roll(tile, NFFT, 1)
            first, second = tile[:HALF], lane_halves_swapped(tile[HALF:], lane)
            both = first + jnp.where(lane < HALF, second, -second)
            gram_out[j] = jnp.where(
                half_low, both[: HALF // 2], pltpu.roll(both[HALF // 2 :], NFFT, 1)
            )

            @pl.when(j != me)
            def _():
                pltpu.make_async_remote_copy(
                    gram_out.at[j], gram_in.at[me], g_send, g_recv,
                    device_id={"tm": j}, device_id_type=MESH,
                ).start()

            @pl.when(j == me)
            def _():
                pltpu.make_async_copy(gram_out.at[j], gram_in.at[me], g_recv).start()

    pltpu.make_async_copy(gram_in, gram_in, g_recv).wait()
    total[row] = jnp.sum(gram_in[...], axis=0)
    for step in range(1, n_space):
        pltpu.make_async_remote_copy(
            total.at[row], total.at[row], y_send, y_recv,
            device_id={"space": lax.rem(row + step, n_space)}, device_id_type=MESH,
        ).start()
    others = total.at[pl.ds(0, n_space - 1)]
    pltpu.make_async_copy(others, others, y_recv).wait()
    packed = total[0]
    for step in range(1, n_space):
        packed = packed + total[step]
    packed = packed * scale

    near = jnp.concatenate([packed, pltpu.roll(packed, NFFT, 1)], axis=0)
    near = jnp.where(low, near, 0.0)
    top = jnp.where(lane < HALF, near, -near)
    bottom = jnp.where(low, lane_halves_swapped(near, lane), 0.0)
    matrix = jnp.concatenate([top, bottom], axis=0)
    empty = jnp.zeros((NFFT, 128), jnp.float32)
    column = lax.broadcasted_iota(jnp.int32, (NFFT, 128), 1)

    def applied(v):
        return jnp.dot(
            matrix, jnp.concatenate([v, empty], axis=0),
            precision=lax.Precision.HIGHEST, preferred_element_type=jnp.float32,
        )

    vec = start[...]
    for _ in range(SWEEPS):
        vec = applied(vec)
        for k in range(MODES):
            new = jnp.broadcast_to(vec[:, k : k + 1], (NFFT, 128))
            new = new / jnp.sqrt(jnp.sum(new * new, axis=0, keepdims=True))
            inner_re = jnp.sum(new * vec, axis=0, keepdims=True)
            inner_im = jnp.sum(new * turned(vec), axis=0, keepdims=True)
            less = vec - (inner_re * new - inner_im * turned(new))
            vec = jnp.where(column == k, new, jnp.where(column > k, less, vec))
    vec = jnp.where(column < MODES, vec, 0.0)

    wide = lax.broadcasted_iota(jnp.int32, (8, 128), 1)
    flat = jnp.concatenate([vec * factor, empty], axis=0).T[:8]
    real_rows = jnp.where(wide < HALF, flat, -flat)
    imag_rows = jnp.where(wide < NFFT, lane_halves_swapped(flat, wide), 0.0)
    lines = jnp.concatenate(
        [rows[k : k + 1] for k in range(MODES) for rows in (real_rows, imag_rows)], axis=0
    )
    lines = jnp.where(lax.rem(me, 2) == 1, pltpu.roll(lines, NFFT, 1), lines)

    mine[...] = lines.astype(jnp.bfloat16)
    for offset in PEERS:
        pltpu.make_async_remote_copy(
            mine, mix.at[me], m_send, m_recv.at[home],
            device_id={"tm": peer_of(me, offset)}, device_id_type=MESH,
        ).start()
    pltpu.make_async_copy(mine, mix.at[me], m_recv.at[home]).start()
    energies[...] = jnp.sum(vec * applied(vec), axis=0, keepdims=True)[:, :MODES]

    span = pl.ds(pl.multiple_of(me * own, own), own)
    for step in GROUP_ORDER:
        g = lax.rem(home + step, GROUPS)
        four = mix.at[pl.ds(g * IN_GROUP, IN_GROUP)]
        pltpu.make_async_copy(four, four, m_recv.at[g]).wait()
        zero = jnp.zeros((8, 128), jnp.float32)
        rows = [mix[g * IN_GROUP + f].astype(jnp.float32) for f in range(IN_GROUP)]
        rows = [
            jnp.concatenate([line, zero] if f < 2 else [zero, line], axis=1)
            for f, line in enumerate(rows)
        ]
        rows = jnp.concatenate(rows, axis=0).astype(jnp.bfloat16)
        for part in range(parts):
            made = jnp.dot(rows, spec[g, part], preferred_element_type=jnp.float32)
            made = made.astype(jnp.bfloat16)
            for c in range(COMP):
                piece = made[:, c * width : (c + 1) * width]
                here = slice(part * width, (part + 1) * width)
                for f in range(IN_GROUP):
                    for k in range(MODES):
                        out_buf[g * IN_GROUP + f, k * COMP + c, :, here] = piece[
                            f * 8 + 2 * k : f * 8 + 2 * k + 2
                        ]
        for f in range(IN_GROUP):
            j = g * IN_GROUP + f

            @pl.when(j != me)
            def _():
                pltpu.make_async_remote_copy(
                    out_buf.at[j], modes.at[:, :, span], o_send, o_recv,
                    device_id={"tm": j}, device_id_type=MESH,
                ).start()

            @pl.when(j == me)
            def _():
                pltpu.make_async_copy(out_buf.at[j], modes.at[:, :, span], o_recv).start()

    sent = x_buf.at[:, :, pl.ds(0, (NF - 1) * HALF), :]
    for part in range(parts):
        pltpu.make_async_copy(sent.at[part], sent.at[part], x_send.at[part]).wait()
    others = gram_out.at[pl.ds(0, NF - 1)]
    pltpu.make_async_copy(others, others, g_send).wait()
    others = total.at[pl.ds(0, n_space - 1)]
    pltpu.make_async_copy(others, others, y_send).wait()
    others = mix.at[pl.ds(0, NF - 1)]
    pltpu.make_async_copy(others, others, m_send).wait()
    others = out_buf.at[pl.ds(0, NF - 1)]
    pltpu.make_async_copy(others, others, o_send).wait()
    pltpu.make_async_copy(out_buf, out_buf, o_recv).wait()


def hand_over(energies, modes, energies_out, modes_out, sem):
    give = pltpu.make_async_copy(modes, modes_out, sem)
    give.start()
    energies_out[...] = energies[...]
    give.wait()


def per_device(table, energy_sum, snapshots, cell_weights, freq_order):
    n_tm = lax.axis_size("tm")
    cells = snapshots.shape[2]
    own = cells // n_tm
    parts = 8
    width = own // parts
    scale = 1.0 / (energy_sum * COMP * cells * lax.axis_size("space"))
    factor = 1.0 / math.sqrt(energy_sum)
    snaps = jnp.transpose(snapshots, (1, 0, 2))
    weights = cell_weights.reshape(n_tm, own // 128, 128)
    dma = pltpu.SemaphoreType.DMA
    vmem = pl.BlockSpec(memory_space=pltpu.VMEM)
    far = pl.BlockSpec(memory_space=pl.ANY)
    energies, modes = pl.pallas_call(
        functools.partial(kernel, parts, width, scale, factor),
        out_shape=(
            pltpu.VMEM((1, MODES), jnp.float32),
            pltpu.VMEM((MODES * COMP, 2, cells), jnp.bfloat16),
        ),
        in_specs=[far] * 5,
        out_specs=(vmem, vmem),
        scratch_shapes=[
            pltpu.SMEM((NF,), jnp.int32),
            pltpu.VMEM((NF, 8, 128), jnp.float32),
            pltpu.VMEM((2 * HALF, 128), jnp.float32),
            pltpu.VMEM((own // 128, 128), jnp.float32),
            pltpu.VMEM((parts, COMP, n_tm * HALF, width), jnp.bfloat16),
            pltpu.VMEM((STRIP_ROWS, 2 * STRIP), jnp.bfloat16),
            pltpu.VMEM((STRIP_ROWS, STRIP), jnp.bfloat16),
            pltpu.VMEM((STRIPS, STRIP_ROWS, COMP * width), jnp.float32),
            pltpu.VMEM((GROUPS, parts, GROUP_ROWS, COMP * width), jnp.bfloat16),
            pltpu.VMEM((GROUPS, GROUP_ROWS, GROUP_ROWS), jnp.float32),
            pltpu.VMEM((NF, HALF // 2, 128), jnp.float32),
            pltpu.VMEM((n_tm, HALF // 2, 128), jnp.float32),
            pltpu.VMEM((lax.axis_size("space"), HALF // 2, 128), jnp.float32),
            pltpu.VMEM((2 * MODES, 128), jnp.bfloat16),
            pltpu.VMEM((NF, 2 * MODES, 128), jnp.bfloat16),
            pltpu.VMEM((NF, MODES * COMP, 2, own), jnp.bfloat16),
            dma((4,)),
            dma((parts,)),
            dma((parts,)),
            dma,
            dma,
            dma,
            dma,
            dma,
            dma((GROUPS,)),
            dma,
            dma,
        ],
        compiler_params=pltpu.CompilerParams(
            collective_id=0, has_side_effects=True, vmem_limit_bytes=56 << 20
        ),
        name="spod",
    )(freq_order, snaps, weights, table, first_vectors())
    energies, modes = pl.pallas_call(
        hand_over,
        out_shape=(
            jax.ShapeDtypeStruct(energies.shape, energies.dtype),
            jax.ShapeDtypeStruct(modes.shape, modes.dtype),
        ),
        in_specs=[vmem, vmem],
        out_specs=(vmem, far),
        scratch_shapes=[dma],
        name="hand_over",
    )(*(pltpu.with_memory_space_constraint(x, pltpu.VMEM) for x in (energies, modes)))
    modes = modes.reshape(MODES, COMP, 2, cells).transpose(0, 2, 1, 3)
    return energies, modes[None]


def solution(mesh):
    table, energy_sum = basis_rows()
    rounded = table.astype(jnp.bfloat16).astype(np.float32)
    return jax.shard_map(
        functools.partial(per_device, rounded, energy_sum),
        mesh=mesh,
        in_specs=(P("tm", None, "space"), P("space"), P()),
        out_specs=(P("tm", None), P("tm", None, None, None, "space")),
        check_vma=False,
    )
```

```python
import functools
import math

import jax
import jax.numpy as jnp
import numpy as np
from jax import lax
from jax.experimental import pallas as pl
from jax.experimental.pallas import tpu as pltpu
from jax.sharding import PartitionSpec as P

NFFT = 64
COMP = 3
MODES = 4
SWEEPS = 3
HALF = 32
NF = 32
NB = 31
SHIFT = 0.61
MESH = pl.DeviceIdType.MESH

CYCLE = (0, 1, 2, 3)
PEERS = [
    (CYCLE[(turn + lead) % 4], dx, dc)
    for dc in (0, 1)
    for turn in range(4)
    for dx, lead in ((2, 0), (1, 1), (3, 3), (0, 2))
    if (CYCLE[(turn + lead) % 4], dx, dc) != (0, 0, 0)
]
GROUPS = 8
IN_GROUP = NF // GROUPS
GROUP_ROWS = IN_GROUP * 2 * HALF
GROUP_ORDER = (5, 2, 7, 4, 1, 6, 3, 0)
STRIP = 8 * HALF
STRIPS = 4
STRIP_ROWS = 8 * 2 * NF


def peer_of(me, offset):
    z, x, core = me // 8, (me // 2) % 4, me % 2
    return (((z + offset[0]) % 4) * 4 + (x + offset[1]) % 4) * 2 + (core + offset[2]) % 2


def basis_rows():
    sample = np.arange(NFFT)
    freqs = np.arange(NF)
    turn = ((freqs[:, None] * sample[None, :]) % NFFT).astype(np.float32)
    angle = np.float32(2.0 * math.pi) * turn / np.float32(NFFT)
    hann_angle = np.float32(2.0 * math.pi) * sample.astype(np.float32) / np.float32(NFFT)
    hann = np.float32(0.5) - np.float32(0.5) * np.cos(hann_angle)
    basis = np.stack([hann * np.cos(angle), -hann * np.sin(angle)], 1)
    even = np.concatenate([basis, basis], 2)
    odd = np.concatenate([basis[:, :, HALF:], basis, basis[:, :, :HALF]], 2)
    table = np.zeros((NF, 8, 128), np.float32)
    table[:, 0:2] = even
    table[:, 2:4] = odd
    return table, float(np.sum(hann * hann))


def first_vectors():
    rows = np.arange(NB, dtype=np.float32)[:, None] + np.float32(1.0)
    cols = np.arange(MODES, dtype=np.float32)[None, :] + np.float32(1.0)
    table = np.zeros((2 * HALF, 128), np.float32)
    table[:NB, :MODES] = np.cos(np.float32(SHIFT) * rows * cols)
    return table


def turned(y):
    return jnp.concatenate([y[HALF:], -y[:HALF]], axis=0)


def lane_halves_swapped(x, lane):
    return jnp.where(lane < HALF, shifted(x, -HALF), shifted(x, HALF))


def shifted(x, lanes):
    return pltpu.roll(x, lanes % 128, 1) if lanes % 128 else x


def kernel(
    parts, width, scale, factor,
    order_far, snaps, weights, table_far, start_far, energies, modes,
    order, table, start, w_buf, x_buf, dft, dft_end, fresh, spec, gram,
    gram_out, gram_in, total, mine, mix, out_buf,
    load_sem, x_send, x_recv, g_send, g_recv, y_send, y_recv, m_send, m_recv, o_send, o_recv,
):
    me = lax.axis_index("tm")
    row = lax.axis_index("space")
    n_space = lax.axis_size("space")
    own = parts * width
    last_part = parts - 1
    home = me // IN_GROUP

    barrier = pltpu.get_barrier_semaphore()
    for offset in PEERS:
        pl.semaphore_signal(
            barrier, inc=1, device_id={"tm": peer_of(me, offset)}, device_id_type=MESH
        )
    for step in range(1, n_space):
        pl.semaphore_signal(
            barrier, inc=1, device_id={"space": lax.rem(row + step, n_space)}, device_id_type=MESH
        )
    loads = [
        pltpu.make_async_copy(far, near, load_sem.at[k])
        for k, (far, near) in enumerate(
            ((order_far, order), (table_far, table), (start_far, start), (weights.at[me], w_buf))
        )
    ]
    for load in loads:
        load.start()
    pl.semaphore_wait(barrier, len(PEERS) + n_space - 1)

    def source(owner, part):
        at = pl.multiple_of(owner * own + part * width, width)
        return snaps.at[:, :, pl.ds(at, width)]

    def landing(part, chunk):
        return x_buf.at[part, :, pl.ds(pl.multiple_of(chunk * HALF, HALF), HALF), :]

    @pl.loop(0, parts)
    def _(part):
        for offset in PEERS:
            peer = peer_of(me, offset)
            pltpu.make_async_remote_copy(
                source(peer, part), landing(part, me), x_send.at[part], x_recv.at[part],
                device_id={"tm": peer}, device_id_type=MESH,
            ).start()
        pltpu.make_async_copy(source(me, part), landing(part, me), x_recv.at[part]).start()

    block = lax.broadcasted_iota(jnp.int32, (8, 2 * STRIP), 0)
    since = lax.broadcasted_iota(jnp.int32, (8, 2 * STRIP), 1) - HALF * block
    inside = (since >= 0) & (since < NFFT)
    use_even = inside & (block % 2 == 0)
    use_odd = inside & (block % 2 == 1)
    present = (block < 7)[:, :STRIP]
    for load in loads:
        load.wait()

    @pl.loop(0, NF)
    def _(j):
        rows = table[order[j]]
        bands = []
        for r in range(2):
            even = jnp.broadcast_to(jnp.tile(rows[r : r + 1], (1, 4)), (8, 2 * STRIP))
            odd = jnp.broadcast_to(jnp.tile(rows[r + 2 : r + 3], (1, 4)), (8, 2 * STRIP))
            bands.append(jnp.where(use_even, even, jnp.where(use_odd, odd, 0.0)))
        at = pl.ds(pl.multiple_of(j * 16, 16), 16)
        dft[at, :] = jnp.concatenate(bands, axis=0).astype(jnp.bfloat16)
        bands = [jnp.where(present, band[:, :STRIP], 0.0) for band in bands]
        dft_end[at, :] = jnp.concatenate(bands, axis=0).astype(jnp.bfloat16)

    gram[...] = jnp.zeros_like(gram)

    def transform(part):
        pltpu.make_async_copy(x_buf.at[part], x_buf.at[part], x_recv.at[part]).wait()
        for strip in range(STRIPS):
            last = strip == STRIPS - 1
            rows = slice(strip * STRIP, (strip + 1 if last else strip + 2) * STRIP)
            given = jnp.concatenate([x_buf[part, c, rows] for c in range(COMP)], axis=1)
            fresh[strip] = jnp.dot(
                (dft_end if last else dft)[...], given, preferred_element_type=jnp.float32
            )

    def accumulate(part, g):
        pieces = [fresh[k, pl.ds(pl.multiple_of(g * 64, 64), 64), :] for k in range(STRIPS)]
        found = jnp.concatenate(
            [piece[line * 8 : line * 8 + 8] for line in range(8) for piece in pieces], axis=0
        ).astype(jnp.bfloat16)
        spec[g, part] = found
        scales = jnp.tile(w_buf[pl.ds(part, 1), :], (1, COMP))
        heavy = (found.astype(jnp.float32) * scales).astype(jnp.bfloat16)
        gram[g] += lax.dot_general(
            heavy, found, (((1,), (1,)), ((), ())), preferred_element_type=jnp.float32
        )

    @pl.loop(0, last_part)
    def _(part):
        transform(part)

        @pl.loop(0, GROUPS)
        def _(g):
            accumulate(part, g)

    lane = lax.broadcasted_iota(jnp.int32, (HALF, 128), 1)
    line = lax.broadcasted_iota(jnp.int32, (HALF, 128), 0)
    quarter = lax.broadcasted_iota(jnp.int32, (8, 128), 1) // HALF
    transform(last_part)

    @pl.loop(0, GROUPS)
    def _(step):
        g = lax.rem(home + 5 * (step + 1), GROUPS)
        accumulate(last_part, g)
        for f in range(IN_GROUP):
            j = g * IN_GROUP + f
            tile = gram[g, f * NFFT : (f + 1) * NFFT, (f // 2) * 128 : (f // 2 + 1) * 128]
            base = (f % 2) * NFFT
            first, second = tile[:HALF], tile[HALF:]
            real_part = first + shifted(second, -HALF)
            imag_part = shifted(first, -HALF) - second
            both = jnp.where(lane - base >= line, real_part, imag_part)
            piece = both[:8]
            piece = shifted(piece, -base)
            for q in range(1, 4):
                more = shifted(both[q * 8 : q * 8 + 8], q * HALF - base)
                piece = jnp.where(quarter == q, more, piece)
            gram_out[j] = piece

            @pl.when(j != me)
            def _():
                pltpu.make_async_remote_copy(
                    gram_out.at[j], gram_in.at[me], g_send, g_recv,
                    device_id={"tm": j}, device_id_type=MESH,
                ).start()

            @pl.when(j == me)
            def _():
                pltpu.make_async_copy(gram_out.at[j], gram_in.at[me], g_recv).start()

    pltpu.make_async_copy(gram_in, gram_in, g_recv).wait()
    total[row] = jnp.sum(gram_in[...], axis=0)
    for step in range(1, n_space):
        pltpu.make_async_remote_copy(
            total.at[row], total.at[row], y_send, y_recv,
            device_id={"space": lax.rem(row + step, n_space)}, device_id_type=MESH,
        ).start()
    others = total.at[pl.ds(0, n_space - 1)]
    pltpu.make_async_copy(others, others, y_recv).wait()
    packed = total[0]
    for step in range(1, n_space):
        packed = packed + total[step]
    packed = packed * scale

    both = jnp.concatenate([shifted(packed, -q * HALF) for q in range(4)], axis=0)
    both = jnp.where(lane < HALF, both, 0.0)
    across = jnp.concatenate([both, jnp.zeros((128 - HALF, 128), jnp.float32)], axis=0).T[:HALF]
    real_part = jnp.where(lane >= line, both, across)
    imag_part = jnp.where(lane < line, both, jnp.where(lane > line, -across, 0.0))
    top = real_part - shifted(imag_part, HALF)
    bottom = imag_part + shifted(real_part, HALF)
    matrix = jnp.concatenate([top, bottom], axis=0)
    empty = jnp.zeros((NFFT, 128), jnp.float32)
    column = lax.broadcasted_iota(jnp.int32, (NFFT, 128), 1)

    def applied(v):
        return jnp.dot(
            matrix, jnp.concatenate([v, empty], axis=0),
            precision=lax.Precision.HIGHEST, preferred_element_type=jnp.float32,
        )

    vec = start[...]
    for _ in range(SWEEPS):
        vec = applied(vec)
        for k in range(MODES):
            raw = jnp.broadcast_to(vec[:, k : k + 1], (NFFT, 128))
            square = jnp.sum(raw * raw, axis=0, keepdims=True)
            if k < MODES - 1:
                inner_re = jnp.sum(raw * vec, axis=0, keepdims=True) / square
                inner_im = jnp.sum(raw * turned(vec), axis=0, keepdims=True) / square
                less = vec - (inner_re * raw - inner_im * turned(raw))
                vec = jnp.where(column > k, less, vec)
            vec = jnp.where(column == k, raw / jnp.sqrt(square), vec)
    vec = jnp.where(column < MODES, vec, 0.0)

    wide = lax.broadcasted_iota(jnp.int32, (8, 128), 1)
    flat = jnp.concatenate([vec * factor, empty], axis=0).T[:8]
    real_rows = jnp.where(wide < HALF, flat, -flat)
    imag_rows = jnp.where(wide < NFFT, lane_halves_swapped(flat, wide), 0.0)
    lines = jnp.concatenate(
        [rows[k : k + 1] for k in range(MODES) for rows in (real_rows, imag_rows)], axis=0
    )
    lines = jnp.where(lax.rem(me, 2) == 1, pltpu.roll(lines, NFFT, 1), lines)

    mine[...] = lines.astype(jnp.bfloat16)
    for offset in PEERS:
        pltpu.make_async_remote_copy(
            mine, mix.at[me], m_send, m_recv.at[home],
            device_id={"tm": peer_of(me, offset)}, device_id_type=MESH,
        ).start()
    pltpu.make_async_copy(mine, mix.at[me], m_recv.at[home]).start()
    energies[...] = jnp.sum(vec * applied(vec), axis=0, keepdims=True)[:, :MODES]

    span = pl.ds(pl.multiple_of(me * own, own), own)
    for step in GROUP_ORDER:
        g = lax.rem(home + step, GROUPS)
        four = mix.at[pl.ds(g * IN_GROUP, IN_GROUP)]
        pltpu.make_async_copy(four, four, m_recv.at[g]).wait()
        zero = jnp.zeros((8, 128), jnp.float32)
        rows = [mix[g * IN_GROUP + f].astype(jnp.float32) for f in range(IN_GROUP)]
        rows = [
            jnp.concatenate([line, zero] if f < 2 else [zero, line], axis=1)
            for f, line in enumerate(rows)
        ]
        rows = jnp.concatenate(rows, axis=0).astype(jnp.bfloat16)
        for part in range(parts):
            made = jnp.dot(rows, spec[g, part], preferred_element_type=jnp.float32)
            made = made.astype(jnp.bfloat16)
            for c in range(COMP):
                piece = made[:, c * width : (c + 1) * width]
                here = slice(part * width, (part + 1) * width)
                for f in range(IN_GROUP):
                    for k in range(MODES):
                        out_buf[g * IN_GROUP + f, k * COMP + c, :, here] = piece[
                            f * 8 + 2 * k : f * 8 + 2 * k + 2
                        ]
        for f in range(IN_GROUP):
            j = g * IN_GROUP + f

            @pl.when(j != me)
            def _():
                pltpu.make_async_remote_copy(
                    out_buf.at[j], modes.at[:, :, span], o_send, o_recv,
                    device_id={"tm": j}, device_id_type=MESH,
                ).start()

            @pl.when(j == me)
            def _():
                pltpu.make_async_copy(out_buf.at[j], modes.at[:, :, span], o_recv).start()

    sent = x_buf.at[:, :, pl.ds(0, (NF - 1) * HALF), :]
    for part in range(parts):
        pltpu.make_async_copy(sent.at[part], sent.at[part], x_send.at[part]).wait()
    others = gram_out.at[pl.ds(0, NF - 1)]
    pltpu.make_async_copy(others, others, g_send).wait()
    others = total.at[pl.ds(0, n_space - 1)]
    pltpu.make_async_copy(others, others, y_send).wait()
    others = mix.at[pl.ds(0, NF - 1)]
    pltpu.make_async_copy(others, others, m_send).wait()
    others = out_buf.at[pl.ds(0, NF - 1)]
    pltpu.make_async_copy(others, others, o_send).wait()
    pltpu.make_async_copy(out_buf, out_buf, o_recv).wait()


def hand_over(energies, modes, energies_out, modes_out, sem):
    give = pltpu.make_async_copy(modes, modes_out, sem)
    give.start()
    energies_out[...] = energies[...]
    give.wait()


def per_device(table, energy_sum, snapshots, cell_weights, freq_order):
    n_tm = lax.axis_size("tm")
    cells = snapshots.shape[2]
    own = cells // n_tm
    parts = 8
    width = own // parts
    scale = 1.0 / (energy_sum * COMP * cells * lax.axis_size("space"))
    factor = 1.0 / math.sqrt(energy_sum)
    snaps = jnp.transpose(snapshots, (1, 0, 2))
    weights = cell_weights.reshape(n_tm, own // 128, 128)
    dma = pltpu.SemaphoreType.DMA
    vmem = pl.BlockSpec(memory_space=pltpu.VMEM)
    far = pl.BlockSpec(memory_space=pl.ANY)
    energies, modes = pl.pallas_call(
        functools.partial(kernel, parts, width, scale, factor),
        out_shape=(
            pltpu.VMEM((1, MODES), jnp.float32),
            pltpu.VMEM((MODES * COMP, 2, cells), jnp.bfloat16),
        ),
        in_specs=[far] * 5,
        out_specs=(vmem, vmem),
        scratch_shapes=[
            pltpu.SMEM((NF,), jnp.int32),
            pltpu.VMEM((NF, 8, 128), jnp.float32),
            pltpu.VMEM((2 * HALF, 128), jnp.float32),
            pltpu.VMEM((own // 128, 128), jnp.float32),
            pltpu.VMEM((parts, COMP, n_tm * HALF, width), jnp.bfloat16),
            pltpu.VMEM((STRIP_ROWS, 2 * STRIP), jnp.bfloat16),
            pltpu.VMEM((STRIP_ROWS, STRIP), jnp.bfloat16),
            pltpu.VMEM((STRIPS, STRIP_ROWS, COMP * width), jnp.float32),
            pltpu.VMEM((GROUPS, parts, GROUP_ROWS, COMP * width), jnp.bfloat16),
            pltpu.VMEM((GROUPS, GROUP_ROWS, GROUP_ROWS), jnp.float32),
            pltpu.VMEM((NF, 8, 128), jnp.float32),
            pltpu.VMEM((n_tm, 8, 128), jnp.float32),
            pltpu.VMEM((lax.axis_size("space"), 8, 128), jnp.float32),
            pltpu.VMEM((2 * MODES, 128), jnp.bfloat16),
            pltpu.VMEM((NF, 2 * MODES, 128), jnp.bfloat16),
            pltpu.VMEM((NF, MODES * COMP, 2, own), jnp.bfloat16),
            dma((4,)),
            dma((parts,)),
            dma((parts,)),
            dma,
            dma,
            dma,
            dma,
            dma,
            dma((GROUPS,)),
            dma,
            dma,
        ],
        compiler_params=pltpu.CompilerParams(
            collective_id=0, has_side_effects=True, vmem_limit_bytes=56 << 20
        ),
        name="spod",
    )(freq_order, snaps, weights, table, first_vectors())
    energies, modes = pl.pallas_call(
        hand_over,
        out_shape=(
            jax.ShapeDtypeStruct(energies.shape, energies.dtype),
            jax.ShapeDtypeStruct(modes.shape, modes.dtype),
        ),
        in_specs=[vmem, vmem],
        out_specs=(vmem, far),
        scratch_shapes=[dma],
        name="hand_over",
    )(*(pltpu.with_memory_space_constraint(x, pltpu.VMEM) for x in (energies, modes)))
    modes = modes.reshape(MODES, COMP, 2, cells).transpose(0, 2, 1, 3)
    return energies, modes[None]


def solution(mesh):
    table, energy_sum = basis_rows()
    rounded = table.astype(jnp.bfloat16).astype(np.float32)
    return jax.shard_map(
        functools.partial(per_device, rounded, energy_sum),
        mesh=mesh,
        in_specs=(P("tm", None, "space"), P("space"), P()),
        out_specs=(P("tm", None), P("tm", None, None, None, "space")),
        check_vma=False,
    )
```

```python
import functools
import math

import jax
import jax.numpy as jnp
import numpy as np
from jax import lax
from jax.experimental import pallas as pl
from jax.experimental.pallas import tpu as pltpu
from jax.sharding import PartitionSpec as P

NFFT = 64
COMP = 3
MODES = 4
SWEEPS = 3
HALF = 32
NF = 32
NB = 31
SHIFT = 0.61
MESH = pl.DeviceIdType.MESH

CYCLE = (0, 1, 2, 3)
PEERS = [
    (CYCLE[(turn + lead) % 4], dx, dc)
    for dc in (0, 1)
    for turn in range(4)
    for dx, lead in ((2, 0), (1, 1), (3, 3), (0, 2))
    if (CYCLE[(turn + lead) % 4], dx, dc) != (0, 0, 0)
]
GROUPS = 8
IN_GROUP = NF // GROUPS
GROUP_ROWS = IN_GROUP * 2 * HALF
STRIP = 8 * HALF
STRIPS = 4
STRIP_ROWS = 8 * 2 * NF


def peer_of(me, offset):
    z, x, core = me // 8, (me // 2) % 4, me % 2
    return (((z + offset[0]) % 4) * 4 + (x + offset[1]) % 4) * 2 + (core + offset[2]) % 2


def basis_rows():
    sample = np.arange(NFFT)
    freqs = np.arange(NF)
    turn = ((freqs[:, None] * sample[None, :]) % NFFT).astype(np.float32)
    angle = np.float32(2.0 * math.pi) * turn / np.float32(NFFT)
    hann_angle = np.float32(2.0 * math.pi) * sample.astype(np.float32) / np.float32(NFFT)
    hann = np.float32(0.5) - np.float32(0.5) * np.cos(hann_angle)
    basis = np.stack([hann * np.cos(angle), -hann * np.sin(angle)], 1)
    even = np.concatenate([basis, basis], 2)
    odd = np.concatenate([basis[:, :, HALF:], basis, basis[:, :, :HALF]], 2)
    table = np.zeros((NF, 8, 128), np.float32)
    table[:, 0:2] = even
    table[:, 2:4] = odd
    return table, float(np.sum(hann * hann))


def first_vectors():
    rows = np.arange(NB, dtype=np.float32)[:, None] + np.float32(1.0)
    cols = np.arange(MODES, dtype=np.float32)[None, :] + np.float32(1.0)
    table = np.zeros((2 * HALF, 128), np.float32)
    table[:NB, :MODES] = np.cos(np.float32(SHIFT) * rows * cols)
    return table


def turned(y):
    return jnp.concatenate([y[HALF:], -y[:HALF]], axis=0)


def lane_halves_swapped(x, lane):
    return jnp.where(lane < HALF, shifted(x, -HALF), shifted(x, HALF))


def shifted(x, lanes):
    return pltpu.roll(x, lanes % 128, 1) if lanes % 128 else x


def kernel(
    parts, width, scale, factor,
    order_far, snaps, weights, table_far, start_far, energies, modes,
    order, table, start, w_buf, x_buf, dft, dft_end, fresh, spec, gram,
    gram_out, gram_in, total, mine, mix, out_buf,
    load_sem, x_send, x_recv, g_send, g_recv, y_send, y_recv, m_send, m_recv, o_send, o_recv,
):
    me = lax.axis_index("tm")
    row = lax.axis_index("space")
    n_space = lax.axis_size("space")
    own = parts * width
    last_part = parts - 1
    home = me // IN_GROUP

    barrier = pltpu.get_barrier_semaphore()
    for offset in PEERS:
        pl.semaphore_signal(
            barrier, inc=1, device_id={"tm": peer_of(me, offset)}, device_id_type=MESH
        )
    for step in range(1, n_space):
        pl.semaphore_signal(
            barrier, inc=1, device_id={"space": lax.rem(row + step, n_space)}, device_id_type=MESH
        )
    loads = [
        pltpu.make_async_copy(far, near, load_sem.at[k])
        for k, (far, near) in enumerate(
            ((order_far, order), (table_far, table), (start_far, start), (weights.at[me], w_buf))
        )
    ]
    for load in loads:
        load.start()
    pl.semaphore_wait(barrier, len(PEERS) + n_space - 1)

    def source(owner, part):
        at = pl.multiple_of(owner * own + part * width, width)
        return snaps.at[:, :, pl.ds(at, width)]

    def landing(part, chunk):
        return x_buf.at[part, :, pl.ds(pl.multiple_of(chunk * HALF, HALF), HALF), :]

    @pl.loop(0, parts)
    def _(part):
        for offset in PEERS:
            peer = peer_of(me, offset)
            pltpu.make_async_remote_copy(
                source(peer, part), landing(part, me), x_send.at[part], x_recv.at[part],
                device_id={"tm": peer}, device_id_type=MESH,
            ).start()
        pltpu.make_async_copy(source(me, part), landing(part, me), x_recv.at[part]).start()

    block = lax.broadcasted_iota(jnp.int32, (8, 2 * STRIP), 0)
    since = lax.broadcasted_iota(jnp.int32, (8, 2 * STRIP), 1) - HALF * block
    inside = (since >= 0) & (since < NFFT)
    use_even = inside & (block % 2 == 0)
    use_odd = inside & (block % 2 == 1)
    present = (block < 7)[:, :STRIP]
    for load in loads:
        load.wait()

    @pl.loop(0, NF)
    def _(j):
        rows = table[order[j]]
        bands = []
        for r in range(2):
            even = jnp.broadcast_to(jnp.tile(rows[r : r + 1], (1, 4)), (8, 2 * STRIP))
            odd = jnp.broadcast_to(jnp.tile(rows[r + 2 : r + 3], (1, 4)), (8, 2 * STRIP))
            bands.append(jnp.where(use_even, even, jnp.where(use_odd, odd, 0.0)))
        at = pl.ds(pl.multiple_of(j * 16, 16), 16)
        dft[at, :] = jnp.concatenate(bands, axis=0).astype(jnp.bfloat16)
        bands = [jnp.where(present, band[:, :STRIP], 0.0) for band in bands]
        dft_end[at, :] = jnp.concatenate(bands, axis=0).astype(jnp.bfloat16)

    gram[...] = jnp.zeros_like(gram)

    def transform(part):
        pltpu.make_async_copy(x_buf.at[part], x_buf.at[part], x_recv.at[part]).wait()
        for strip in range(STRIPS):
            last = strip == STRIPS - 1
            rows = slice(strip * STRIP, (strip + 1 if last else strip + 2) * STRIP)
            given = jnp.concatenate([x_buf[part, c, rows] for c in range(COMP)], axis=1)
            fresh[strip] = jnp.dot(
                (dft_end if last else dft)[...], given, preferred_element_type=jnp.float32
            )

    def accumulate(part, g):
        pieces = [fresh[k, pl.ds(pl.multiple_of(g * 64, 64), 64), :] for k in range(STRIPS)]
        found = jnp.concatenate(
            [piece[line * 8 : line * 8 + 8] for line in range(8) for piece in pieces], axis=0
        ).astype(jnp.bfloat16)
        spec[g, part] = found
        scales = jnp.tile(w_buf[pl.ds(part, 1), :], (1, COMP))
        heavy = (found.astype(jnp.float32) * scales).astype(jnp.bfloat16)
        gram[g] += lax.dot_general(
            heavy, found, (((1,), (1,)), ((), ())), preferred_element_type=jnp.float32
        )

    @pl.loop(0, last_part)
    def _(part):
        transform(part)

        @pl.loop(0, GROUPS)
        def _(g):
            accumulate(part, g)

    lane = lax.broadcasted_iota(jnp.int32, (HALF, 128), 1)
    line = lax.broadcasted_iota(jnp.int32, (HALF, 128), 0)
    quarter = lax.broadcasted_iota(jnp.int32, (8, 128), 1) // HALF
    transform(last_part)

    @pl.loop(0, GROUPS)
    def _(step):
        g = lax.rem(home + 5 * (step + 1), GROUPS)
        accumulate(last_part, g)
        for f in range(IN_GROUP):
            j = g * IN_GROUP + f
            tile = gram[g, f * NFFT : (f + 1) * NFFT, (f // 2) * 128 : (f // 2 + 1) * 128]
            base = (f % 2) * NFFT
            first, second = tile[:HALF], tile[HALF:]
            real_part = first + shifted(second, -HALF)
            imag_part = shifted(first, -HALF) - second
            both = jnp.where(lane - base >= line, real_part, imag_part)
            piece = both[:8]
            piece = shifted(piece, -base)
            for q in range(1, 4):
                more = shifted(both[q * 8 : q * 8 + 8], q * HALF - base)
                piece = jnp.where(quarter == q, more, piece)
            gram_out[j] = piece

            @pl.when(j != me)
            def _():
                pltpu.make_async_remote_copy(
                    gram_out.at[j], gram_in.at[me], g_send, g_recv,
                    device_id={"tm": j}, device_id_type=MESH,
                ).start()

            @pl.when(j == me)
            def _():
                pltpu.make_async_copy(gram_out.at[j], gram_in.at[me], g_recv).start()

    pltpu.make_async_copy(gram_in, gram_in, g_recv).wait()
    total[row] = jnp.sum(gram_in[...], axis=0)
    for step in range(1, n_space):
        pltpu.make_async_remote_copy(
            total.at[row], total.at[row], y_send, y_recv,
            device_id={"space": lax.rem(row + step, n_space)}, device_id_type=MESH,
        ).start()
    others = total.at[pl.ds(0, n_space - 1)]
    pltpu.make_async_copy(others, others, y_recv).wait()
    packed = total[0]
    for step in range(1, n_space):
        packed = packed + total[step]
    packed = packed * scale

    both = jnp.concatenate([shifted(packed, -q * HALF) for q in range(4)], axis=0)
    both = jnp.where(lane < HALF, both, 0.0)
    across = jnp.concatenate([both, jnp.zeros((128 - HALF, 128), jnp.float32)], axis=0).T[:HALF]
    real_part = jnp.where(lane >= line, both, across)
    imag_part = jnp.where(lane < line, both, jnp.where(lane > line, -across, 0.0))
    top = real_part - shifted(imag_part, HALF)
    bottom = imag_part + shifted(real_part, HALF)
    matrix = jnp.concatenate([top, bottom], axis=0)
    empty = jnp.zeros((NFFT, 128), jnp.float32)
    column = lax.broadcasted_iota(jnp.int32, (NFFT, 128), 1)

    def applied(v):
        return jnp.dot(
            matrix, jnp.concatenate([v, empty], axis=0),
            precision=lax.Precision.HIGHEST, preferred_element_type=jnp.float32,
        )

    vec = start[...]
    for _ in range(SWEEPS):
        vec = applied(vec)
        for k in range(MODES):
            raw = jnp.broadcast_to(vec[:, k : k + 1], (NFFT, 128))
            square = jnp.sum(raw * raw, axis=0, keepdims=True)
            if k < MODES - 1:
                inner_re = jnp.sum(raw * vec, axis=0, keepdims=True) / square
                inner_im = jnp.sum(raw * turned(vec), axis=0, keepdims=True) / square
                less = vec - (inner_re * raw - inner_im * turned(raw))
                vec = jnp.where(column > k, less, vec)
            vec = jnp.where(column == k, raw / jnp.sqrt(square), vec)
    vec = jnp.where(column < MODES, vec, 0.0)

    wide = lax.broadcasted_iota(jnp.int32, (8, 128), 1)
    flat = jnp.concatenate([vec * factor, empty], axis=0).T[:8]
    real_rows = jnp.where(wide < HALF, flat, -flat)
    imag_rows = jnp.where(wide < NFFT, lane_halves_swapped(flat, wide), 0.0)
    lines = jnp.concatenate(
        [rows[k : k + 1] for k in range(MODES) for rows in (real_rows, imag_rows)], axis=0
    )
    lines = jnp.where(lax.rem(me, 2) == 1, pltpu.roll(lines, NFFT, 1), lines)

    mine[...] = lines.astype(jnp.bfloat16)
    for offset in PEERS:
        pltpu.make_async_remote_copy(
            mine, mix.at[me], m_send, m_recv.at[home],
            device_id={"tm": peer_of(me, offset)}, device_id_type=MESH,
        ).start()
    pltpu.make_async_copy(mine, mix.at[me], m_recv.at[home]).start()
    energies[...] = jnp.sum(vec * applied(vec), axis=0, keepdims=True)[:, :MODES]

    sent = x_buf.at[:, :, pl.ds(0, (NF - 1) * HALF), :]
    for part in range(parts):
        pltpu.make_async_copy(sent.at[part], sent.at[part], x_send.at[part]).wait()
    others = gram_out.at[pl.ds(0, NF - 1)]
    pltpu.make_async_copy(others, others, g_send).wait()
    others = total.at[pl.ds(0, n_space - 1)]
    pltpu.make_async_copy(others, others, y_send).wait()

    span = pl.ds(pl.multiple_of(me * own, own), own)
    @pl.loop(0, GROUPS)
    def _(step):
        g = lax.rem(home + 5 * (step + 1), GROUPS)
        four = mix.at[pl.ds(g * IN_GROUP, IN_GROUP)]
        pltpu.make_async_copy(four, four, m_recv.at[g]).wait()
        zero = jnp.zeros((8, 128), jnp.float32)
        rows = [mix[g * IN_GROUP + f].astype(jnp.float32) for f in range(IN_GROUP)]
        rows = [
            jnp.concatenate([line, zero] if f < 2 else [zero, line], axis=1)
            for f, line in enumerate(rows)
        ]
        rows = jnp.concatenate(rows, axis=0).astype(jnp.bfloat16)
        for part in range(parts):
            made = jnp.dot(rows, spec[g, part], preferred_element_type=jnp.float32)
            made = made.astype(jnp.bfloat16)
            for c in range(COMP):
                piece = made[:, c * width : (c + 1) * width]
                here = slice(part * width, (part + 1) * width)
                for f in range(IN_GROUP):
                    for k in range(MODES):
                        out_buf[g * IN_GROUP + f, k * COMP + c, :, here] = piece[
                            f * 8 + 2 * k : f * 8 + 2 * k + 2
                        ]
        for f in range(IN_GROUP):
            j = g * IN_GROUP + f

            @pl.when(j != me)
            def _():
                pltpu.make_async_remote_copy(
                    out_buf.at[j], modes.at[:, :, span], o_send, o_recv,
                    device_id={"tm": j}, device_id_type=MESH,
                ).start()

            @pl.when(j == me)
            def _():
                pltpu.make_async_copy(out_buf.at[j], modes.at[:, :, span], o_recv).start()

    others = mix.at[pl.ds(0, NF - 1)]
    pltpu.make_async_copy(others, others, m_send).wait()
    others = out_buf.at[pl.ds(0, NF - 1)]
    pltpu.make_async_copy(others, others, o_send).wait()
    pltpu.make_async_copy(out_buf, out_buf, o_recv).wait()


def hand_over(energies, modes, energies_out, modes_out, sem):
    gives = [
        pltpu.make_async_copy(modes.at[k], modes_out.at[k], sem.at[k])
        for k in range(modes.shape[0])
    ]
    for give in gives:
        give.start()
    energies_out[...] = energies[...]
    for give in gives:
        give.wait()


def per_device(table, energy_sum, snapshots, cell_weights, freq_order):
    n_tm = lax.axis_size("tm")
    cells = snapshots.shape[2]
    own = cells // n_tm
    parts = 8
    width = own // parts
    scale = 1.0 / (energy_sum * COMP * cells * lax.axis_size("space"))
    factor = 1.0 / math.sqrt(energy_sum)
    snaps = jnp.transpose(snapshots, (1, 0, 2))
    weights = cell_weights.reshape(n_tm, own // 128, 128)
    dma = pltpu.SemaphoreType.DMA
    vmem = pl.BlockSpec(memory_space=pltpu.VMEM)
    far = pl.BlockSpec(memory_space=pl.ANY)
    energies, modes = pl.pallas_call(
        functools.partial(kernel, parts, width, scale, factor),
        out_shape=(
            pltpu.VMEM((1, MODES), jnp.float32),
            pltpu.VMEM((MODES * COMP, 2, cells), jnp.bfloat16),
        ),
        in_specs=[far] * 5,
        out_specs=(vmem, vmem),
        scratch_shapes=[
            pltpu.SMEM((NF,), jnp.int32),
            pltpu.VMEM((NF, 8, 128), jnp.float32),
            pltpu.VMEM((2 * HALF, 128), jnp.float32),
            pltpu.VMEM((own // 128, 128), jnp.float32),
            pltpu.VMEM((parts, COMP, n_tm * HALF, width), jnp.bfloat16),
            pltpu.VMEM((STRIP_ROWS, 2 * STRIP), jnp.bfloat16),
            pltpu.VMEM((STRIP_ROWS, STRIP), jnp.bfloat16),
            pltpu.VMEM((STRIPS, STRIP_ROWS, COMP * width), jnp.float32),
            pltpu.VMEM((GROUPS, parts, GROUP_ROWS, COMP * width), jnp.bfloat16),
            pltpu.VMEM((GROUPS, GROUP_ROWS, GROUP_ROWS), jnp.float32),
            pltpu.VMEM((NF, 8, 128), jnp.float32),
            pltpu.VMEM((n_tm, 8, 128), jnp.float32),
            pltpu.VMEM((lax.axis_size("space"), 8, 128), jnp.float32),
            pltpu.VMEM((2 * MODES, 128), jnp.bfloat16),
            pltpu.VMEM((NF, 2 * MODES, 128), jnp.bfloat16),
            pltpu.VMEM((NF, MODES * COMP, 2, own), jnp.bfloat16),
            dma((4,)),
            dma((parts,)),
            dma((parts,)),
            dma,
            dma,
            dma,
            dma,
            dma,
            dma((GROUPS,)),
            dma,
            dma,
        ],
        compiler_params=pltpu.CompilerParams(
            collective_id=0, has_side_effects=True, vmem_limit_bytes=56 << 20
        ),
        name="spod",
    )(freq_order, snaps, weights, table, first_vectors())
    energies, modes = pl.pallas_call(
        hand_over,
        out_shape=(
            jax.ShapeDtypeStruct(energies.shape, energies.dtype),
            jax.ShapeDtypeStruct(modes.shape, modes.dtype),
        ),
        in_specs=[vmem, vmem],
        out_specs=(vmem, far),
        scratch_shapes=[dma((MODES * COMP,))],
        name="hand_over",
    )(*(pltpu.with_memory_space_constraint(x, pltpu.VMEM) for x in (energies, modes)))
    modes = modes.reshape(MODES, COMP, 2, cells).transpose(0, 2, 1, 3)
    return energies, modes[None]


def solution(mesh):
    table, energy_sum = basis_rows()
    rounded = table.astype(jnp.bfloat16).astype(np.float32)
    return jax.shard_map(
        functools.partial(per_device, rounded, energy_sum),
        mesh=mesh,
        in_specs=(P("tm", None, "space"), P("space"), P()),
        out_specs=(P("tm", None), P("tm", None, None, None, "space")),
        check_vma=False,
    )
```
